512 devices in a mesh: ctx: 64 (over z_lo, y, core), head: 8 (over z_hi, x).
Axes of the slice: x: 4, y: 8, z: 8 (z_hi: 2, z_lo: 4; z = z_hi * 4 + z_lo), core: 2. Of those that a mesh axis runs over, the one named last changes fastest.
Arguments:
- frozen_queries: bfloat16 [8192, 12288], P('ctx', 'head'), may hold values from -20.4 to 20.4
- query_latent_rows: bfloat16 [8192, 1536], P('ctx'), may hold values from -6 to 6
- key_value_latent: bfloat16 [8192, 576], P('ctx'), may hold values from -20.4 to 20.4
- block_starts: int32 [64, 2], P('ctx'), may hold values from 0 to 960, as said below
- latent_up_weight: bfloat16 [512, 16384], P(None, 'head'), may hold values from -0.25 to 0.25
- query_adapter_first: bfloat16 [1536, 32], replicated, may hold values from -0.15625 to 0.15625
- query_adapter_second: bfloat16 [32, 12288], P(None, 'head'), may hold values from -1 to 1
- output_adapter_first: bfloat16 [8192, 32], P('head'), may hold values from -0.0625 to 0.0625
- output_adapter_second: bfloat16 [32, 2560], replicated, may hold values from -1 to 1
- frozen_output_weight: bfloat16 [8192, 2560], P('head', 'ctx'), may hold values from -0.0625 to 0.0625
- output_cotangent: bfloat16 [8192, 2560], P('ctx'), may hold values from -0.1875 to 0.1875
Outputs:
- grad_qa: float32 [1536, 32], replicated
- grad_qb: float32 [32, 12288], P(None, 'head')
- grad_oa: float32 [8192, 32], P('head')
- grad_ob: float32 [32, 2560], P(None, 'ctx')
The draws below stay inside these ranges and needn't reach their ends.
Inputs may be any that keep to these rules, and one draw needn't show every extreme that they name: For c < 8, each of the 8 groups of one sequence holds block_starts = (c * 64, (15 - c) * 64), every c once per sequence.
All inputs are finite; a program needn't handle non-finite values.
Results may differ from the reference program's by a relative error of at most 0.02.
The reference program's roundings to bfloat16 on the way count: a program that leaves them out, or rounds other values in their place, can miss the bound.
Values may be sent and summed in bfloat16 or wider, within the bound.
A program may use at most 128 MiB of HBM per device.

```python
import jax
import jax.numpy as jnp
from jax import lax

MODEL_WIDTH = 2560
HEAD_TOTAL = 64
PLAIN_WIDTH = 128
ROTARY_WIDTH = 64
VALUE_WIDTH = 128
KVL = 512
QUERY_LATENT = 1536
ADAPTER_RANK = 32
SPAN = 8
TOK_DEV = 128
HALF = 64
SEQS = 8
TOKENS = 8192


def draw_block_starts(key, part):
    seq_keys = jax.random.split(key, SEQS)
    orders = jax.vmap(lambda item: jax.random.permutation(item, SPAN))(seq_keys)
    chosen = orders.T.reshape(SEQS * SPAN).astype(jnp.int32)
    lower = chosen * HALF
    upper = (2 * SPAN - 1 - chosen) * HALF
    return jnp.stack([lower, upper], 1).astype(jnp.int32)


def draw_frozen_queries(key, part):
    per_head_width = PLAIN_WIDTH + ROTARY_WIDTH
    entries = jnp.clip(jax.random.normal(key, (TOKENS, HEAD_TOTAL, per_head_width), jnp.float32), -6.0, 6.0)
    return entries.reshape(TOKENS, HEAD_TOTAL * per_head_width).astype(jnp.bfloat16)


def draw_key_value_latent(key, part):
    entries = jnp.clip(jax.random.normal(key, (TOKENS, KVL + ROTARY_WIDTH), jnp.float32), -6.0, 6.0)
    return entries.astype(jnp.bfloat16)


def spiked(drawn, own_key, source, target, parts, factor):
    owner, partner = [(jnp.arange(drawn.shape[position]) // (drawn.shape[position] // parts)).reshape([-1 if axis == position else 1 for axis in range(drawn.ndim)]) for position in (source, target)]
    chosen = jax.random.permutation(own_key, parts)[partner]
    strong = (owner == chosen) | (owner == (partner + parts // 2) % parts)
    return jnp.where(strong, factor * drawn, drawn)


def levels(key, extent, cuts, least, high):
    gain, own = 1.0, jax.random.fold_in(key, 6)
    for dim, parts in cuts:
        draws = jnp.exp(jax.random.uniform(jax.random.fold_in(own, dim), (parts,), jnp.float32, least / len(cuts), high / len(cuts)))
        gain = gain * jnp.repeat(draws, extent[dim] // parts).reshape([-1 if axis == dim else 1 for axis in range(len(extent))])
    return gain


def scatter_about(own_key, extent, scale, limit, shards=(), held_as=jnp.bfloat16):
    values = jax.random.normal(own_key, extent, jnp.float32) * scale
    if len(shards) > 0:
        values = levels(own_key, extent, shards, -0.22, 0.18) * values
    return jnp.clip(values, min=-limit, max=limit).astype(held_as)


def noise_with(own_key, dims, deviation, most, cuts, heavy, held_as=jnp.bfloat16):
    result = deviation * jax.random.normal(own_key, dims, jnp.float32)
    if cuts:
        result = result * levels(own_key, dims, cuts, -0.22, 0.18)
    return jnp.clip(spiked(result, jax.random.fold_in(own_key, 3), *heavy), -most, most).astype(held_as)


def setup_inputs(seed: int = 0) -> dict:
    seeds = jax.random.split(jax.random.key(seed), 12)
    frozen_queries = draw_frozen_queries(jax.random.fold_in(seeds[11], 71), 0)
    query_latent_rows = scatter_about(seeds[1], (TOKENS, QUERY_LATENT), 1.0, 6.0, ((0, 64),))
    key_value_latent = draw_key_value_latent(jax.random.fold_in(seeds[11], 71), 0)
    block_starts = draw_block_starts(jax.random.fold_in(seeds[11], 71), 0)
    latent_up_weight = scatter_about(seeds[4], (KVL, HEAD_TOTAL * (PLAIN_WIDTH + VALUE_WIDTH)), KVL ** -0.5, 0.25, ((1, 8),))
    query_adapter_first = scatter_about(seeds[5], (QUERY_LATENT, ADAPTER_RANK), QUERY_LATENT ** -0.5, 0.15625)
    query_adapter_second = scatter_about(seeds[6], (ADAPTER_RANK, HEAD_TOTAL * (PLAIN_WIDTH + ROTARY_WIDTH)), ADAPTER_RANK ** -0.5, 1.0, ((1, 8),))
    output_adapter_first = scatter_about(seeds[7], (HEAD_TOTAL * VALUE_WIDTH, ADAPTER_RANK), (HEAD_TOTAL * VALUE_WIDTH) ** -0.5, 0.0625, ((0, 8),))
    output_adapter_second = scatter_about(seeds[8], (ADAPTER_RANK, MODEL_WIDTH), ADAPTER_RANK ** -0.5, 1.0)
    frozen_output_weight = scatter_about(seeds[9], (HEAD_TOTAL * VALUE_WIDTH, MODEL_WIDTH), (HEAD_TOTAL * VALUE_WIDTH) ** -0.5, 0.0625, ((0, 8), (1, 64)))
    output_cotangent = noise_with(seeds[10], (TOKENS, MODEL_WIDTH), (TOKENS ** -0.5), 0.1875, ((0, 64),), (0, 1, 64, 4.0))
    return {"frozen_queries": frozen_queries, "query_latent_rows": query_latent_rows, "key_value_latent": key_value_latent, "block_starts": block_starts, "latent_up_weight": latent_up_weight, "query_adapter_first": query_adapter_first, "query_adapter_second": query_adapter_second, "output_adapter_first": output_adapter_first, "output_adapter_second": output_adapter_second, "frozen_output_weight": frozen_output_weight, "output_cotangent": output_cotangent}


ROPE_BASE = 10000.0


def rotate(vectors, positions, sign):
    half_width = vectors.shape[-1] // 2
    freq = ROPE_BASE ** (-jnp.arange(half_width, dtype=jnp.float32) * 2.0 / vectors.shape[-1])
    angle = positions.astype(jnp.float32)[..., None] * freq
    angle = angle.reshape(positions.shape + (1,) * (vectors.ndim - positions.ndim - 1) + (half_width,))
    cosine = jnp.cos(angle)
    sine = jnp.sin(angle) * sign
    first = vectors[..., :half_width]
    second = vectors[..., half_width:]
    return jnp.concatenate([first * cosine - second * sine, second * cosine + first * sine], -1)


def block_positions(block_starts, half_rows):
    steps = jnp.arange(half_rows, dtype=jnp.int32)
    return (block_starts[:, :, None] + steps).reshape(block_starts.shape[0], 2 * half_rows)


def by_sequence(array):
    rest = array.shape[1:]
    array = array.reshape((SPAN, SEQS, TOK_DEV) + rest)
    array = jnp.moveaxis(array, 1, 0)
    return array.reshape((SEQS, SPAN * TOK_DEV) + rest)


def from_sequence(array):
    rest = array.shape[2:]
    array = array.reshape((SEQS, SPAN, TOK_DEV) + rest)
    array = jnp.moveaxis(array, 0, 1)
    return array.reshape((TOKENS,) + rest)


def attend_sequence(inputs):
    query_full, kv_up, rope_key, positions, attended_gradient = inputs
    per_head_width = PLAIN_WIDTH + ROTARY_WIDTH
    score_scale = per_head_width ** -0.5
    query_full = query_full.astype(jnp.float32)
    key_nope = kv_up[..., :PLAIN_WIDTH].astype(jnp.float32)
    values = kv_up[..., PLAIN_WIDTH:].astype(jnp.float32)
    rope_wide = rope_key.astype(jnp.float32)
    scores = jnp.einsum("qhd,khd->hqk", query_full[..., :PLAIN_WIDTH], key_nope)
    scores = (scores + jnp.einsum("qhd,kd->hqk", query_full[..., PLAIN_WIDTH:], rope_wide)) * score_scale
    causal = positions[None, :] <= positions[:, None]
    scores = jnp.where(causal[None], scores, -jnp.inf)
    top = jnp.max(scores, -1, keepdims=True)
    expo = jnp.exp(scores - top)
    weights = (expo / jnp.sum(expo, -1, keepdims=True)).astype(jnp.bfloat16)
    weights_wide = weights.astype(jnp.float32)
    attended_values = jnp.einsum("hqk,khv->qhv", weights_wide, values).astype(jnp.bfloat16)
    d_prob = jnp.einsum("qhv,khv->hqk", attended_gradient.astype(jnp.float32), values)
    delta = jnp.sum(weights_wide * d_prob, -1, keepdims=True)
    d_score = (weights_wide * (d_prob - delta) * score_scale).astype(jnp.bfloat16).astype(jnp.float32)
    dq_nope = jnp.einsum("hqk,khd->qhd", d_score, key_nope)
    dq_rope = jnp.einsum("hqk,kd->qhd", d_score, rope_wide)
    return attended_values, dq_nope, dq_rope


def reference(frozen_queries, query_latent_rows, key_value_latent, block_starts, latent_up_weight, query_adapter_first, query_adapter_second, output_adapter_first, output_adapter_second, frozen_output_weight, output_cotangent):
    per_head_width = PLAIN_WIDTH + ROTARY_WIDTH
    positions = block_positions(block_starts, TOK_DEV // 2).reshape(TOKENS)
    query_rank_rows = jnp.dot(query_latent_rows, query_adapter_first, preferred_element_type=jnp.float32).astype(jnp.bfloat16)
    query_full = frozen_queries.astype(jnp.float32) + jnp.dot(query_rank_rows, query_adapter_second, preferred_element_type=jnp.float32)
    query_full = query_full.reshape(TOKENS, HEAD_TOTAL, per_head_width)
    query_full = jnp.concatenate([query_full[..., :PLAIN_WIDTH], rotate(query_full[..., PLAIN_WIDTH:], positions, 1.0)], -1).astype(jnp.bfloat16)
    kv_up = jnp.dot(key_value_latent[:, :KVL], latent_up_weight, preferred_element_type=jnp.float32).astype(jnp.bfloat16)
    kv_up = kv_up.reshape(TOKENS, HEAD_TOTAL, PLAIN_WIDTH + VALUE_WIDTH)
    rope_key = rotate(key_value_latent[:, KVL:].astype(jnp.float32), positions, 1.0).astype(jnp.bfloat16)
    output_rank_gradient = jnp.dot(output_cotangent, output_adapter_second.T, preferred_element_type=jnp.float32).astype(jnp.bfloat16)
    attended_gradient = jnp.dot(output_cotangent, frozen_output_weight.T, preferred_element_type=jnp.float32)
    attended_gradient = attended_gradient + jnp.dot(output_rank_gradient, output_adapter_first.T, preferred_element_type=jnp.float32)
    attended_gradient = attended_gradient.astype(jnp.bfloat16).reshape(TOKENS, HEAD_TOTAL, VALUE_WIDTH)
    attended_values, dq_nope, dq_rope = lax.map(attend_sequence, (by_sequence(query_full), by_sequence(kv_up), by_sequence(rope_key), by_sequence(positions), by_sequence(attended_gradient)))
    attended_values = from_sequence(attended_values).reshape(TOKENS, HEAD_TOTAL * VALUE_WIDTH)
    dq_nope = from_sequence(dq_nope)
    dq_rope = rotate(from_sequence(dq_rope), positions, -1.0)
    query_gradient = jnp.concatenate([dq_nope, dq_rope], -1).reshape(TOKENS, HEAD_TOTAL * per_head_width).astype(jnp.bfloat16)
    output_rank_rows = jnp.dot(attended_values, output_adapter_first, preferred_element_type=jnp.float32).astype(jnp.bfloat16)
    grad_ob = jnp.dot(output_rank_rows.T, output_cotangent, preferred_element_type=jnp.float32)
    grad_oa = jnp.dot(attended_values.T, output_rank_gradient, preferred_element_type=jnp.float32)
    grad_qb = jnp.dot(query_rank_rows.T, query_gradient, preferred_element_type=jnp.float32)
    query_adapter_gradient = jnp.dot(query_gradient, query_adapter_second.T, preferred_element_type=jnp.float32).astype(jnp.bfloat16)
    grad_qa = jnp.dot(query_latent_rows.T, query_adapter_gradient, preferred_element_type=jnp.float32)
    return grad_qa, grad_qb, grad_oa, grad_ob
```

```python
import functools

import jax
import jax.numpy as jnp
from jax import lax
from jax.experimental import pallas as pl
from jax.experimental.pallas import tpu as pltpu
from jax.sharding import PartitionSpec as P

PLAIN_WIDTH = 128
ROTARY_WIDTH = 64
VALUE_WIDTH = 128
KVL = 512
SPAN = 8
ROPE_BASE = 10000.0
MESH = pl.DeviceIdType.MESH
VMEM = pltpu.VMEM
DMA = pltpu.SemaphoreType.DMA


def rotate(vectors, positions, sign):
    half_width = vectors.shape[-1] // 2
    freq = ROPE_BASE ** (-jnp.arange(half_width, dtype=jnp.float32) * 2.0 / vectors.shape[-1])
    angle = positions.astype(jnp.float32)[..., None] * freq
    angle = angle.reshape(
        positions.shape + (1,) * (vectors.ndim - positions.ndim - 1) + (half_width,)
    )
    cosine = jnp.cos(angle)
    sine = jnp.sin(angle) * sign
    first = vectors[..., :half_width]
    second = vectors[..., half_width:]
    return jnp.concatenate([first * cosine - second * sine, second * cosine + first * sine], -1)


def block_positions(offsets, half_rows):
    steps = jnp.arange(half_rows, dtype=jnp.int32)
    return jnp.concatenate([offsets[..., :1] + steps, offsets[..., 1:] + steps], -1)


def contract_rows(left, right):
    return lax.dot_general(
        left, right, (((0,), (0,)), ((), ())), preferred_element_type=jnp.float32
    )


def columns_contract(left, right):
    return lax.dot_general(
        left, right, (((1,), (1,)), ((), ())), preferred_element_type=jnp.float32
    )


def send(src, dst, send_sem, recv_sem, axis, target):
    copy = pltpu.make_async_remote_copy(
        src_ref=src,
        dst_ref=dst,
        send_sem=send_sem,
        recv_sem=recv_sem,
        device_id={axis: target},
        device_id_type=MESH,
    )
    copy.start()
    return copy


def greet(axis, targets):
    barrier = pltpu.get_barrier_semaphore()
    for target in targets:
        pl.semaphore_signal(barrier, inc=1, device_id={axis: target}, device_id_type=MESH)
    pl.semaphore_wait(barrier, len(targets))


def places(place):
    core = lax.rem(place, 2)
    y = lax.rem(place // 2, 8)
    z = place // 16
    partner = place + 1 - 2 * core
    return core, y, z, partner


def gather_kernel(
    kv_ref, starts_ref, w_ref, cot_ref,
    kv_out, starts_out, w_out, cot_out,
    local_sem, kv_s, kv_r, st_s, st_r, pair_s, pair_r, z_s, z_r, y_s, y_r,
):
    place = lax.axis_index("ctx")
    core, y, z, partner = places(place)
    slot = place // 8
    kin = [lax.rem(place + 8 * step, 64) for step in range(1, SPAN)]
    up = z * 16 + lax.rem(y + 1, 8) * 2 + core
    down = z * 16 + lax.rem(y + 7, 8) * 2 + core
    greet("ctx", kin + [partner, up, down])

    own = [
        pltpu.make_async_copy(kv_ref, kv_out.at[slot], local_sem.at[0]),
        pltpu.make_async_copy(starts_ref, starts_out.at[slot], local_sem.at[1]),
        pltpu.make_async_copy(w_ref.at[core], w_out.at[z, y, core], local_sem.at[2]),
        pltpu.make_async_copy(cot_ref, cot_out.at[core], local_sem.at[3]),
    ]
    for copy in own:
        copy.start()
    pending = []
    swap_w = send(
        w_ref.at[1 - core], w_out.at[z, y, core], pair_s.at[0], pair_r.at[0], "ctx", partner
    )
    swap_cot = send(cot_ref, cot_out.at[core], pair_s.at[1], pair_r.at[1], "ctx", partner)
    line = []
    for step in range(1, 4):
        target = lax.rem(z + step, 4) * 16 + y * 2 + core
        line.append([
            send(
                w_ref.at[core], w_out.at[z, y, core],
                z_s.at[step - 1, 0], z_r.at[step - 1, 0], "ctx", target,
            )
        ])
    for step in range(1, SPAN):
        pending.append(
            send(starts_ref, starts_out.at[slot], st_s.at[step - 1], st_r.at[step - 1], "ctx", kin[step - 1])
        )
        pending.append(
            send(kv_ref, kv_out.at[slot], kv_s.at[step - 1], kv_r.at[step - 1], "ctx", kin[step - 1])
        )
    swap_w.wait_recv()
    for step in range(1, 4):
        target = lax.rem(z + step, 4) * 16 + y * 2 + core
        line[step - 1].append(
            send(
                w_out.at[z, y, 1 - core], w_out.at[z, y, 1 - core],
                z_s.at[step - 1, 1], z_r.at[step - 1, 1], "ctx", target,
            )
        )
    own[2].wait()
    rings = {}
    for step in range(1, 5):
        for unit in range(4):
            depth = lax.rem(z - unit + 4, 4)
            if step == 1:
                if unit:
                    line[unit - 1][0].wait_recv()
                    line[unit - 1][1].wait_recv()
            for side, target in ((0, up), (1, down)):
                if step > 1:
                    rings[side, step - 1, unit].wait_recv()
                if step == 4 and (unit // 2) != side:
                    continue
                shift = -(step - 1) if side == 0 else step - 1
                column = lax.rem(y + shift + 8, 8)
                rings[side, step, unit] = send(
                    w_out.at[depth, column], w_out.at[depth, column],
                    y_s.at[side, step - 1, unit], y_r.at[side, step - 1, unit], "ctx", target,
                )
    for unit in range(4):
        rings[unit // 2, 4, unit].wait_recv()
    for copy in pending + [swap_cot]:
        copy.wait_recv()
    for copy in pending + [swap_w, swap_cot] + line[0] + line[1] + line[2] + list(rings.values()):
        copy.wait_send()
    own[0].wait()
    own[1].wait()
    own[3].wait()


def swap_kernel(half_ref, out_ref, local_sem, send_sem, recv_sem):
    place = lax.axis_index("ctx")
    core, _, _, partner = places(place)
    greet("ctx", [partner])
    own = pltpu.make_async_copy(half_ref.at[core], out_ref.at[core], local_sem)
    own.start()
    copy = send(half_ref.at[1 - core], out_ref.at[core], send_sem, recv_sem, "ctx", partner)
    copy.wait()
    own.wait()


def head_kernel(part_ref, out_ref, landed, mine, s1, r1, s2, r2):
    place = lax.axis_index("head")
    peers = [lax.rem(place + step, 8) for step in range(1, 8)]
    greet("head", peers)
    copies = [
        send(part_ref.at[peer], landed.at[step], s1.at[step], r1.at[step], "head", peer)
        for step, peer in enumerate(peers)
    ]
    total = part_ref[place]
    for step, copy in enumerate(copies):
        copy.wait_recv()
        total = total + landed[step]
    rounded = total.astype(jnp.bfloat16)
    mine[...] = rounded
    out_ref[place] = rounded
    second = [
        send(mine, out_ref.at[place], s2.at[step], r2.at[step], "head", peer)
        for step, peer in enumerate(peers)
    ]
    for copy in second:
        copy.wait_recv()
    for copy in copies + second:
        copy.wait_send()


def reduce_kernel(
    x_ref, full_ref, tail_ref,
    r1, t1, r2, t2, r3, g0, ga, gy, sems_s, sems_r, local_sem,
):
    place = lax.axis_index("ctx")
    core, y, _, partner = places(place)
    row = lax.rem(y, 4)
    slot = place // 8
    kin = [lax.rem(slot + step, 8) for step in range(1, 8)]
    near = [lax.rem(row + step, 4) for step in range(1, 4)]
    kin_at = [8 * other + lax.rem(place, 8) for other in kin]
    near_at = [8 * slot + 2 * other + core for other in near]
    greet("ctx", kin_at + near_at + [partner])
    sent = []

    def go(index, src, dst, target):
        copy = send(src, dst, sems_s.at[index], sems_r.at[index], "ctx", target)
        sent.append(copy)
        return copy

    go(0, x_ref.at[1 - core], r1, partner).wait_recv()
    t1[...] = (x_ref[core].astype(jnp.float32) + r1[...].astype(jnp.float32)).astype(jnp.bfloat16)
    copies = [go(1 + i, t1.at[near[i]], r2.at[i], near_at[i]) for i in range(3)]
    total = x_ref[core, row].astype(jnp.float32) + r1[row].astype(jnp.float32)
    for i, copy in enumerate(copies):
        copy.wait_recv()
        total = total + r2[i].astype(jnp.float32)
    t2[...] = total.astype(jnp.bfloat16)
    copies = [go(4 + i, t2.at[kin[i]], r3.at[i], kin_at[i]) for i in range(7)]
    total = t2[slot].astype(jnp.float32)
    for i, copy in enumerate(copies):
        copy.wait_recv()
        total = total + r3[i].astype(jnp.float32)
    tail_ref[...] = total[16:]
    lead = total[:16].astype(jnp.bfloat16)
    g0[...] = lead
    ga[slot] = lead
    copies = [go(11 + i, g0, ga.at[slot], kin_at[i]) for i in range(7)]
    for copy in copies:
        copy.wait_recv()
    own = pltpu.make_async_copy(ga, gy.at[row], local_sem.at[0])
    own.start()
    copies = [go(18 + i, ga, gy.at[row], near_at[i]) for i in range(3)]
    for copy in copies:
        copy.wait_recv()
    own.wait()
    last = pltpu.make_async_copy(gy, full_ref.at[core], local_sem.at[1])
    last.start()
    go(21, gy, full_ref.at[core], partner).wait_recv()
    last.wait()
    for copy in sent:
        copy.wait_send()


def call(kernel, out_shape, scratch, ident, *operands):
    count = len(operands)
    specs = [pl.BlockSpec(memory_space=VMEM)]
    outs = jax.tree.map(lambda _: pl.BlockSpec(memory_space=VMEM), out_shape)
    return pl.pallas_call(
        kernel,
        out_shape=out_shape,
        in_specs=specs * count,
        out_specs=outs,
        scratch_shapes=scratch,
        compiler_params=pltpu.CompilerParams(
            collective_id=ident, has_side_effects=True, vmem_limit_bytes=48 * 1024 * 1024
        ),
    )(*operands)


def shaped(shape, dtype=jnp.bfloat16):
    return jax.ShapeDtypeStruct(shape, dtype)


def body(
    frozen_queries,
    query_latent_rows,
    key_value_latent,
    block_starts,
    latent_up_weight,
    query_adapter_first,
    query_adapter_second,
    output_adapter_first,
    output_adapter_second,
    frozen_output_weight,
    output_cotangent,
):
    token_rows = frozen_queries.shape[0]
    half_rows = token_rows // 2
    per_head_width = PLAIN_WIDTH + ROTARY_WIDTH
    head_number = query_adapter_second.shape[1] // per_head_width
    score_scale = per_head_width ** (-0.5)
    width = output_cotangent.shape[1]
    held_rows, held_columns = frozen_output_weight.shape
    half_out = held_rows // 2
    core = lax.rem(lax.axis_index("ctx"), 2)
    own_positions = block_positions(block_starts[0], half_rows)

    rope_key = rotate(key_value_latent[:, KVL:].astype(jnp.float32), own_positions, 1.0)
    kv_sent = jnp.concatenate([key_value_latent[:, :KVL], rope_key.astype(jnp.bfloat16)], -1)
    starts_sent = jnp.pad(block_starts, ((0, 7), (0, 126)))
    w_sent = frozen_output_weight.T.reshape(held_columns, 2, half_out).transpose(1, 0, 2)
    kv_all, starts_all, w_all, cot_pair = call(
        gather_kernel,
        (
            shaped((SPAN,) + kv_sent.shape),
            shaped((SPAN, 8, 128), jnp.int32),
            shaped((4, 8, 2, held_columns, half_out)),
            shaped((2,) + output_cotangent.shape),
        ),
        [
            DMA((4,)), DMA((7,)), DMA((7,)), DMA((7,)), DMA((7,)), DMA((2,)), DMA((2,)),
            DMA((3, 2)), DMA((3, 2)), DMA((2, 4, 4)), DMA((2, 4, 4)),
        ],
        0,
        kv_sent, starts_sent, w_sent, output_cotangent,
    )
    key_count = SPAN * token_rows
    kv_all = kv_all.reshape(key_count, KVL + ROTARY_WIDTH)
    key_positions = block_positions(starts_all[:, 0, :2], half_rows).reshape(key_count)

    cot_both = cot_pair.reshape(2 * token_rows, width)
    rank_both = columns_contract(cot_both, output_adapter_second).astype(jnp.bfloat16)
    adapter_half = lax.dynamic_slice_in_dim(output_adapter_first, core * half_out, half_out, 0)
    d_half = jnp.dot(cot_both, w_all.reshape(width, half_out), preferred_element_type=jnp.float32)
    d_half = (d_half + columns_contract(rank_both, adapter_half)).astype(jnp.bfloat16)
    d_both = call(
        swap_kernel, shaped((2, token_rows, half_out)), [DMA, DMA, DMA], 1,
        d_half.reshape(2, token_rows, half_out),
    )
    attended_gradient = d_both.reshape(2, token_rows, head_number // 2, VALUE_WIDTH)
    attended_gradient = attended_gradient.transpose(0, 2, 1, 3).reshape(
        head_number, token_rows, VALUE_WIDTH
    )
    output_rank_gradient = columns_contract(output_cotangent, output_adapter_second).astype(
        jnp.bfloat16
    )

    query_rank_rows = jnp.dot(
        query_latent_rows, query_adapter_first, preferred_element_type=jnp.float32
    ).astype(jnp.bfloat16)
    query_full = frozen_queries.astype(jnp.float32) + jnp.dot(
        query_rank_rows, query_adapter_second, preferred_element_type=jnp.float32
    )
    query_full = query_full.reshape(token_rows, head_number, per_head_width)
    query_full = jnp.concatenate(
        [query_full[..., :PLAIN_WIDTH], rotate(query_full[..., PLAIN_WIDTH:], own_positions, 1.0)],
        -1,
    ).astype(jnp.bfloat16)

    kv_up = jnp.dot(
        kv_all[:, :KVL], latent_up_weight, preferred_element_type=jnp.float32
    ).astype(jnp.bfloat16)
    rope_keys = kv_all[:, KVL:]
    kv_heads = kv_up.reshape(key_count, head_number, PLAIN_WIDTH + VALUE_WIDTH)
    key_nope = kv_heads[..., :PLAIN_WIDTH]
    values = kv_heads[..., PLAIN_WIDTH:]
    scores = jnp.einsum(
        "qhd,khd->hqk", query_full[..., :PLAIN_WIDTH], key_nope, preferred_element_type=jnp.float32
    ) + jnp.einsum(
        "qhd,kd->hqk", query_full[..., PLAIN_WIDTH:], rope_keys, preferred_element_type=jnp.float32
    )
    causal = key_positions[None, :] <= own_positions[:, None]
    scores = jnp.where(causal[None], scores * score_scale, -jnp.inf)
    top = jnp.max(scores, -1, keepdims=True)
    expo = jnp.exp(scores - top)
    weights = (expo / jnp.sum(expo, -1, keepdims=True)).astype(jnp.bfloat16)
    attended = jnp.einsum(
        "hqk,khv->qhv", weights, values, preferred_element_type=jnp.float32
    ).astype(jnp.bfloat16)
    attended = attended.reshape(token_rows, head_number * VALUE_WIDTH)
    d_prob = jnp.einsum(
        "hqv,khv->hqk", attended_gradient, values, preferred_element_type=jnp.float32
    )
    weights_wide = weights.astype(jnp.float32)
    delta = jnp.sum(weights_wide * d_prob, -1, keepdims=True)
    d_score = (weights_wide * (d_prob - delta) * score_scale).astype(jnp.bfloat16)
    dq_nope = jnp.einsum("hqk,khd->qhd", d_score, key_nope, preferred_element_type=jnp.float32)
    dq_rope = jnp.einsum("hqk,kd->qhd", d_score, rope_keys, preferred_element_type=jnp.float32)
    dq_rope = rotate(dq_rope, own_positions, -1.0)
    query_gradient = (
        jnp.concatenate([dq_nope, dq_rope], -1)
        .reshape(token_rows, head_number * per_head_width)
        .astype(jnp.bfloat16)
    )

    rank = query_adapter_first.shape[1]
    o_part = jnp.dot(attended, output_adapter_first, preferred_element_type=jnp.float32)
    q_part = columns_contract(query_gradient, query_adapter_second)
    part = jnp.concatenate([o_part, q_part, jnp.zeros((token_rows, 128 - 2 * rank), jnp.float32)], -1)
    rows = token_rows // 8
    low = call(
        head_kernel, shaped((8, rows, 128)),
        [
            VMEM((7, rows, 128), jnp.float32), VMEM((rows, 128), jnp.bfloat16),
            DMA((7,)), DMA((7,)), DMA((7,)), DMA((7,)),
        ],
        2, part.reshape(8, rows, 128),
    ).reshape(token_rows, 128)
    output_rank_rows = low[:, :rank]
    query_adapter_gradient = low[:, rank:2 * rank]

    qb_term = contract_rows(query_rank_rows, query_gradient)
    oa_term = contract_rows(output_rank_gradient, attended)
    qa_term = contract_rows(query_adapter_gradient, query_latent_rows)
    ob_term = contract_rows(output_rank_rows, output_cotangent)
    ob_term = ob_term.astype(jnp.bfloat16).reshape(rank, 8, 4, 2, held_columns)
    ob_term = ob_term.transpose(3, 2, 1, 0, 4).reshape(64, -1, 128)
    lead = [term.astype(jnp.bfloat16).reshape(64, -1, 128) for term in (qb_term, oa_term, qa_term)]
    sizes = [term.shape[1] for term in lead]
    pieces = jnp.concatenate(lead + [ob_term], 1)
    pieces = jnp.pad(pieces, ((0, 0), (0, 32 - pieces.shape[1]), (0, 0)))
    bf = jnp.bfloat16
    full, tail = call(
        reduce_kernel,
        (shaped((2, 4, 8, 16, 128)), shaped((16, 128), jnp.float32)),
        [
            VMEM((4, 8, 32, 128), bf), VMEM((4, 8, 32, 128), bf), VMEM((3, 8, 32, 128), bf),
            VMEM((8, 32, 128), bf), VMEM((7, 32, 128), bf), VMEM((16, 128), bf),
            VMEM((8, 16, 128), bf), VMEM((4, 8, 16, 128), bf), DMA((22,)), DMA((22,)), DMA((2,)),
        ],
        3, pieces.reshape(2, 4, 8, 32, 128),
    )
    full = full.reshape(64, 16, 128).astype(jnp.float32)
    first, second = sizes[0], sizes[0] + sizes[1]
    grad_qb = full[:, :first].reshape(qb_term.shape)
    grad_oa = full[:, first:second].reshape(oa_term.shape).T
    grad_qa = full[:, second:].reshape(qa_term.shape).T
    grad_ob = tail[:ob_term.shape[1]].reshape(rank, held_columns)
    return (grad_qa, grad_qb, grad_oa, grad_ob)


def solution(mesh):
    return jax.shard_map(
        body,
        mesh=mesh,
        in_specs=(
            P("ctx", "head"),
            P("ctx", None),
            P("ctx", None),
            P("ctx", None),
            P(None, "head"),
            P(),
            P(None, "head"),
            P("head", None),
            P(),
            P("head", "ctx"),
            P("ctx", None),
        ),
        out_specs=(P(), P(None, "head"), P("head", None), P(None, "ctx")),
        check_vma=False,
    )
```

```python
import functools

import jax
import jax.numpy as jnp
from jax import lax
from jax.experimental import pallas as pl
from jax.experimental.pallas import tpu as pltpu
from jax.sharding import PartitionSpec as P

PLAIN_WIDTH = 128
ROTARY_WIDTH = 64
VALUE_WIDTH = 128
KVL = 512
SPAN = 8
ROPE_BASE = 10000.0
MESH = pl.DeviceIdType.MESH
VMEM = pltpu.VMEM
DMA = pltpu.SemaphoreType.DMA


def block_positions(offsets, half_rows):
    steps = jnp.arange(half_rows, dtype=jnp.int32)
    return jnp.concatenate([offsets[..., :1] + steps, offsets[..., 1:] + steps], -1)


def contract_rows(left, right):
    return lax.dot_general(
        left, right, (((0,), (0,)), ((), ())), preferred_element_type=jnp.float32
    )


def columns_contract(left, right):
    return lax.dot_general(
        left, right, (((1,), (1,)), ((), ())), preferred_element_type=jnp.float32
    )


def send(src, dst, send_sem, recv_sem, axis, target):
    copy = pltpu.make_async_remote_copy(
        src_ref=src,
        dst_ref=dst,
        send_sem=send_sem,
        recv_sem=recv_sem,
        device_id={axis: target},
        device_id_type=MESH,
    )
    copy.start()
    return copy


def greet(axis, targets):
    barrier = pltpu.get_barrier_semaphore()
    for target in targets:
        pl.semaphore_signal(barrier, inc=1, device_id={axis: target}, device_id_type=MESH)
    pl.semaphore_wait(barrier, len(targets))


def places(place):
    core = lax.rem(place, 2)
    y = lax.rem(place // 2, 8)
    z = place // 16
    partner = place + 1 - 2 * core
    return core, y, z, partner


def rows_contract(left, right):
    return lax.dot_general(
        left, right, (((0,), (0,)), ((), ())), preferred_element_type=jnp.float32
    )


def dot(left, right):
    return jnp.dot(left, right, preferred_element_type=jnp.float32)


def turned(vectors, cosine, sine):
    lane = lax.broadcasted_iota(jnp.int32, vectors.shape, 1)
    other = jnp.where(
        lax.rem(lane, 64) < 32, pltpu.roll(vectors, 96, 1), pltpu.roll(vectors, 32, 1)
    )
    return vectors * cosine + other * sine


def attend_kernel(
    kv_ref, places_ref, w_ref, cot_ref, fqn_ref, fqr_ref, own_pos_ref, cos_ref, sin_ref,
    ql_ref, qa_ref, qbn_ref, qbr_ref, oa_ref, ob_ref, up_ref,
    o_out, q_out, qbn_out, qbr_out, oat_out,
    kv_all, place_all, w_all, cot_all, d_mine, d_all,
    qn_s, qr_s, low_s, kcat_s, val_s, wt_s, att_s, gn_s, gr_s,
    local_sem, kv_s, kv_r, st_s, st_r, pair_s, pair_r, z_s, z_r, y_s, y_r, x_s, x_r, f_s, f_r,
):
    place = lax.axis_index("ctx")
    core, y, z, partner = places(place)
    slot = place // 8
    head = lax.axis_index("head")
    x, block = lax.rem(head, 4), (head // 4) * 4
    right, left = block + lax.rem(x + 1, 4), block + lax.rem(x + 3, 4)
    kin = [lax.rem(place + 8 * step, 64) for step in range(1, SPAN)]
    up = z * 16 + lax.rem(y + 1, 8) * 2 + core
    down = z * 16 + lax.rem(y + 7, 8) * 2 + core
    barrier = pltpu.get_barrier_semaphore()
    for target in kin + [partner, up, down]:
        pl.semaphore_signal(barrier, inc=1, device_id={"ctx": target}, device_id_type=MESH)
    for target in (right, left):
        pl.semaphore_signal(barrier, inc=1, device_id={"head": target}, device_id_type=MESH)
    pl.semaphore_wait(barrier, len(kin) + 5)

    own = [
        pltpu.make_async_copy(kv_ref.at[x], kv_all.at[slot, x], local_sem.at[0]),
        pltpu.make_async_copy(places_ref, place_all.at[slot], local_sem.at[1]),
        pltpu.make_async_copy(w_ref.at[core], w_all.at[z, y, core], local_sem.at[2]),
        pltpu.make_async_copy(cot_ref, cot_all.at[core], local_sem.at[3]),
    ]
    for copy in own:
        copy.start()
    pending = []
    swap_w = send(
        w_ref.at[1 - core], w_all.at[z, y, core], pair_s.at[0], pair_r.at[0], "ctx", partner
    )
    first = []
    for step in range(1, SPAN):
        i = step - 1
        first.append(send(kv_ref.at[x], kv_all.at[slot, x], kv_s.at[i], kv_r.at[i], "ctx", kin[i]))
    for i in range(SPAN - 1):
        pending.append(
            send(places_ref, place_all.at[slot], st_s.at[i], st_r.at[i], "ctx", kin[i])
        )
    swap_cot = send(cot_ref, cot_all.at[core], pair_s.at[1], pair_r.at[1], "ctx", partner)
    pending.append(swap_cot)
    across = [
        [
            send(kv_ref.at[x], kv_all.at[slot, x], x_s.at[side, 0], x_r.at[side, 0], "head", target)
        ]
        for side, target in ((0, right), (1, left))
    ]
    line = []
    for step in range(1, 4):
        target = lax.rem(z + step, 4) * 16 + y * 2 + core
        line.append([
            send(
                w_ref.at[core], w_all.at[z, y, core],
                z_s.at[step - 1, 0], z_r.at[step - 1, 0], "ctx", target,
            )
        ])

    low_s[...] = dot(ql_ref[...], qa_ref[...]).astype(jnp.bfloat16)
    qn_s[...] = (fqn_ref[...].astype(jnp.float32) + dot(low_s[...], qbn_ref[...])).astype(
        jnp.bfloat16
    )
    for pair in range(4):
        lanes = slice(128 * pair, 128 * pair + 128)
        vectors = fqr_ref[:, lanes].astype(jnp.float32) + dot(low_s[...], qbr_ref[:, lanes])
        qr_s[:, lanes] = turned(vectors, cos_ref[...], sin_ref[...]).astype(jnp.bfloat16)

    swap_w.wait_recv()
    for step in range(1, 4):
        target = lax.rem(z + step, 4) * 16 + y * 2 + core
        line[step - 1].append(
            send(
                w_all.at[z, y, 1 - core], w_all.at[z, y, 1 - core],
                z_s.at[step - 1, 1], z_r.at[step - 1, 1], "ctx", target,
            )
        )
    own[2].wait()
    rings = {}

    def ring(step, unit):
        depth = lax.rem(z - unit + 4, 4)
        if step == 1 and unit:
            line[unit - 1][0].wait_recv()
            line[unit - 1][1].wait_recv()
        for side, target in ((0, up), (1, down)):
            if step > 1 and (side, step - 1, unit) in rings:
                rings[side, step - 1, unit].wait_recv()
            if step == 5 or (step == 4 and (unit // 2) != side):
                continue
            shift = -(step - 1) if side == 0 else step - 1
            column = lax.rem(y + shift + 8, 8)
            rings[side, step, unit] = send(
                w_all.at[depth, column], w_all.at[depth, column],
                y_s.at[side, step - 1, unit], y_r.at[side, step - 1, unit], "ctx", target,
            )

    ring(1, 0)
    for i in range(SPAN - 1):
        first[i].wait_recv()
        source = lax.rem(slot + 7 - i, 8)
        for side, target in ((0, right), (1, left)):
            across[side].append(
                send(
                    kv_all.at[source, x], kv_all.at[source, x],
                    x_s.at[side, i + 1], x_r.at[side, i + 1], "head", target,
                )
            )
    for unit in range(1, 4):
        ring(1, unit)
    relays = []
    for i in range(SPAN):
        source = lax.rem(slot + 8 - i, 8)
        across[0][i].wait_recv()
        across[1][i].wait_recv()
        if i % 2 == 0:
            target, lane = right, lax.rem(x + 3, 4)
        else:
            target, lane = left, lax.rem(x + 1, 4)
        relays.append(
            send(
                kv_all.at[source, lane], kv_all.at[source, lane],
                f_s.at[i], f_r.at[i], "head", target,
            )
        )
    for unit in range(4):
        ring(2, unit)
    own[0].wait()
    own[1].wait()
    for copy in relays + pending[:SPAN - 1]:
        copy.wait_recv()

    positions = jnp.concatenate([place_all[i, 0:1, :] for i in range(SPAN)], 1)
    keys = positions.shape[1]
    visible = positions <= own_pos_ref[...]
    latents = kv_all[...].reshape(keys, 640)
    rope2 = latents[:, KVL:]
    scale = (PLAIN_WIDTH + ROTARY_WIDTH) ** (-0.5)
    lane_half = lax.broadcasted_iota(jnp.int32, (qr_s.shape[0], 128), 1) // 64

    def forward(number, total):
        kv = dot(latents[:, :KVL], up_ref[:, pl.ds(pl.multiple_of(number * 256, 256), 256)])
        kv = kv.astype(jnp.bfloat16)
        kcat_s[number, :, :128] = kv[:, :128]
        kcat_s[number, :, 128:] = rope2
        val_s[number] = kv[:, 128:]
        plain = qn_s[:, pl.ds(pl.multiple_of(number * 128, 128), 128)]
        turn = qr_s[:, pl.ds(pl.multiple_of((number // 2) * 128, 128), 128)].astype(jnp.float32)
        turn = jnp.where(lane_half == lax.rem(number, 2), turn, 0.0).astype(jnp.bfloat16)
        query = jnp.concatenate([plain, turn], 1)
        scores = columns_contract(query, kcat_s[number]) * scale
        scores = jnp.where(visible, scores, -jnp.inf)
        expo = jnp.exp(scores - jnp.max(scores, -1, keepdims=True))
        weights = (expo / jnp.sum(expo, -1, keepdims=True)).astype(jnp.bfloat16)
        wt_s[number] = weights
        attended = dot(weights, val_s[number]).astype(jnp.bfloat16)
        att_s[:, pl.ds(pl.multiple_of(number * 128, 128), 128)] = attended
        return total + dot(attended, oa_ref[pl.ds(pl.multiple_of(number * 128, 128), 128), :])

    total = jnp.zeros(o_out.shape, jnp.float32)
    for part in range(4):
        total = lax.fori_loop(2 * part, 2 * part + 2, forward, total)
        if part < 3:
            for unit in range(4):
                ring(part + 3, unit)
    o_out[...] = total
    swap_cot.wait_recv()
    own[3].wait()

    tokens, half_out = d_mine.shape[1], d_mine.shape[2]
    cot = cot_all[...].reshape(2 * tokens, cot_all.shape[2])
    rank = columns_contract(cot, ob_ref[...]).astype(jnp.bfloat16)
    d_half = dot(cot, w_all[...].reshape(cot.shape[1], half_out)) + columns_contract(
        rank, oa_ref[pl.ds(pl.multiple_of(core * half_out, half_out), half_out), :]
    )
    d_mine[...] = d_half.astype(jnp.bfloat16).reshape(d_mine.shape)
    swap_d = send(
        d_mine.at[1 - core], d_all.at[core], pair_s.at[2], pair_r.at[2], "ctx", partner
    )
    keep = pltpu.make_async_copy(d_mine.at[core], d_all.at[core], local_sem.at[4])
    keep.start()
    rank_own = columns_contract(cot_ref[...], ob_ref[...]).astype(jnp.bfloat16)
    oat_out[...] = rows_contract(rank_own, att_s[...]).astype(jnp.bfloat16)
    swap_d.wait_recv()
    keep.wait()

    def backward(pair, total):
        turns = []
        for even in range(2):
            number = 2 * pair + even
            lanes = pl.ds(pl.multiple_of(lax.rem(number, 4) * 128, 128), 128)
            d_prob = columns_contract(d_all[number // 4, :, lanes], val_s[number])
            weights = wt_s[number].astype(jnp.float32)
            delta = jnp.sum(weights * d_prob, -1, keepdims=True)
            d_score = (weights * (d_prob - delta) * scale).astype(jnp.bfloat16)
            grad = dot(d_score, kcat_s[number])
            plain = grad[:, :128].astype(jnp.bfloat16)
            at = pl.ds(pl.multiple_of(number * 128, 128), 128)
            gn_s[:, at] = plain
            total = total + columns_contract(plain, qbn_ref[:, at])
            turns.append(turned(grad[:, 128:], cos_ref[...], -sin_ref[...]))
        turn = jnp.where(lane_half == 0, turns[0], turns[1]).astype(jnp.bfloat16)
        at = pl.ds(pl.multiple_of(pair * 128, 128), 128)
        gr_s[:, at] = turn
        return total + columns_contract(turn, qbr_ref[:, at])

    q_out[...] = lax.fori_loop(0, 4, backward, jnp.zeros(q_out.shape, jnp.float32))
    qbn_out[...] = rows_contract(low_s[...], gn_s[...]).astype(jnp.bfloat16)
    qbr_out[...] = rows_contract(low_s[...], gr_s[...]).astype(jnp.bfloat16)

    done = first + pending + [swap_w, swap_d] + line[0] + line[1] + line[2]
    for copy in done + across[0] + across[1] + relays + list(rings.values()):
        copy.wait_send()


def head_kernel(part_ref, out_ref, landed, mine, s1, r1, s2, r2):
    place = lax.axis_index("head")
    peers = [lax.rem(place + step, 8) for step in range(1, 8)]
    greet("head", peers)
    copies = [
        send(part_ref.at[peer], landed.at[step], s1.at[step], r1.at[step], "head", peer)
        for step, peer in enumerate(peers)
    ]
    total = part_ref[place]
    for step, copy in enumerate(copies):
        copy.wait_recv()
        total = total + landed[step]
    rounded = total.astype(jnp.bfloat16)
    mine[...] = rounded
    out_ref[place] = rounded
    second = [
        send(mine, out_ref.at[place], s2.at[step], r2.at[step], "head", peer)
        for step, peer in enumerate(peers)
    ]
    for copy in second:
        copy.wait_recv()
    for copy in copies + second:
        copy.wait_send()


def reduce_kernel(
    x_ref, full_ref, tail_ref,
    r1, t1, r2, t2, r3, g0, ga, gy, sems_s, sems_r, local_sem,
):
    place = lax.axis_index("ctx")
    core, y, _, partner = places(place)
    row = lax.rem(y, 4)
    slot = place // 8
    kin = [lax.rem(slot + step, 8) for step in range(1, 8)]
    near = [lax.rem(row + step, 4) for step in range(1, 4)]
    kin_at = [8 * other + lax.rem(place, 8) for other in kin]
    near_at = [8 * slot + 2 * other + core for other in near]
    greet("ctx", kin_at + near_at + [partner])
    sent = []

    def go(index, src, dst, target):
        copy = send(src, dst, sems_s.at[index], sems_r.at[index], "ctx", target)
        sent.append(copy)
        return copy

    go(0, x_ref.at[1 - core], r1, partner).wait_recv()
    t1[...] = (x_ref[core].astype(jnp.float32) + r1[...].astype(jnp.float32)).astype(jnp.bfloat16)
    copies = [go(1 + i, t1.at[near[i]], r2.at[i], near_at[i]) for i in range(3)]
    total = x_ref[core, row].astype(jnp.float32) + r1[row].astype(jnp.float32)
    for i, copy in enumerate(copies):
        copy.wait_recv()
        total = total + r2[i].astype(jnp.float32)
    t2[...] = total.astype(jnp.bfloat16)
    copies = [go(4 + i, t2.at[kin[i]], r3.at[i], kin_at[i]) for i in range(7)]
    total = t2[slot].astype(jnp.float32)
    for i, copy in enumerate(copies):
        copy.wait_recv()
        total = total + r3[i].astype(jnp.float32)
    tail_ref[...] = total[16:]
    lead = total[:16].astype(jnp.bfloat16)
    g0[...] = lead
    ga[slot] = lead
    copies = [go(11 + i, g0, ga.at[slot], kin_at[i]) for i in range(7)]
    for copy in copies:
        copy.wait_recv()
    own = pltpu.make_async_copy(ga, gy.at[row], local_sem.at[0])
    own.start()
    copies = [go(18 + i, ga, gy.at[row], near_at[i]) for i in range(3)]
    for copy in copies:
        copy.wait_recv()
    own.wait()
    last = pltpu.make_async_copy(gy, full_ref.at[core], local_sem.at[1])
    last.start()
    go(21, gy, full_ref.at[core], partner).wait_recv()
    last.wait()
    for copy in sent:
        copy.wait_send()


def call(kernel, out_shape, scratch, ident, *operands):
    count = len(operands)
    specs = [pl.BlockSpec(memory_space=VMEM)]
    outs = jax.tree.map(lambda _: pl.BlockSpec(memory_space=VMEM), out_shape)
    return pl.pallas_call(
        kernel,
        out_shape=out_shape,
        in_specs=specs * count,
        out_specs=outs,
        scratch_shapes=scratch,
        compiler_params=pltpu.CompilerParams(
            collective_id=ident, has_side_effects=True, vmem_limit_bytes=48 * 1024 * 1024
        ),
    )(*operands)


def shaped(shape, dtype=jnp.bfloat16):
    return jax.ShapeDtypeStruct(shape, dtype)


def body(
    frozen_queries,
    query_latent_rows,
    key_value_latent,
    block_starts,
    latent_up_weight,
    query_adapter_first,
    query_adapter_second,
    output_adapter_first,
    output_adapter_second,
    frozen_output_weight,
    output_cotangent,
):
    token_rows = frozen_queries.shape[0]
    half_rows = token_rows // 2
    per_head_width = PLAIN_WIDTH + ROTARY_WIDTH
    head_number = query_adapter_second.shape[1] // per_head_width
    width = output_cotangent.shape[1]
    rank = query_adapter_first.shape[1]
    held_rows, held_columns = frozen_output_weight.shape
    half_out = held_rows // 2
    bf = jnp.bfloat16
    own_positions = block_positions(block_starts[0], half_rows)

    lane = jnp.arange(128, dtype=jnp.int32)
    freq = ROPE_BASE ** (-(lane % 32).astype(jnp.float32) * 2.0 / ROTARY_WIDTH)
    angle = own_positions.astype(jnp.float32)[:, None] * freq[None, :]
    cosine = jnp.cos(angle)
    sine = jnp.where(lane[None, :] % 64 < 32, -jnp.sin(angle), jnp.sin(angle))
    raw = key_value_latent[:, KVL:].astype(jnp.float32)
    other = jnp.concatenate([raw[:, 32:], raw[:, :32]], 1)
    rope_key = (
        jnp.concatenate([raw, raw], 1) * cosine + jnp.concatenate([other, other], 1) * sine
    ).astype(bf)
    kv_sent = jnp.concatenate([key_value_latent[:, :KVL], rope_key], -1)
    places_sent = jnp.broadcast_to(own_positions[None, :], (8, token_rows))
    w_sent = frozen_output_weight.T.reshape(held_columns, 2, half_out).transpose(1, 0, 2)

    def parted(array):
        split = array.reshape(array.shape[0], head_number, per_head_width)
        return (
            split[..., :PLAIN_WIDTH].reshape(array.shape[0], -1),
            split[..., PLAIN_WIDTH:].reshape(array.shape[0], -1),
        )

    fqn, fqr = parted(frozen_queries)
    qbn, qbr = parted(query_adapter_second)
    keys = SPAN * token_rows
    plain, turn = fqn.shape[1], fqr.shape[1]
    o_part, q_part, qbn_term, qbr_term, oa_term = call(
        attend_kernel,
        (
            shaped((token_rows, rank), jnp.float32),
            shaped((token_rows, rank), jnp.float32),
            shaped((rank, plain)),
            shaped((rank, turn)),
            shaped((rank, held_rows)),
        ),
        [
            VMEM((SPAN, 4, token_rows // 4, 640), bf), VMEM((SPAN, 8, 128), jnp.int32),
            VMEM((4, 8, 2, held_columns, half_out), bf), VMEM((2, token_rows, width), bf),
            VMEM((2, token_rows, half_out), bf), VMEM((2, token_rows, half_out), bf),
            VMEM((token_rows, plain), bf), VMEM((token_rows, turn), bf),
            VMEM((token_rows, rank), bf), VMEM((head_number, keys, 256), bf),
            VMEM((head_number, keys, 128), bf), VMEM((head_number, token_rows, keys), bf),
            VMEM((token_rows, held_rows), bf), VMEM((token_rows, plain), bf),
            VMEM((token_rows, turn), bf),
            DMA((5,)), DMA((7,)), DMA((7,)), DMA((7,)), DMA((7,)), DMA((3,)), DMA((3,)),
            DMA((3, 2)), DMA((3, 2)), DMA((2, 4, 4)), DMA((2, 4, 4)), DMA((2, 8)), DMA((2, 8)),
            DMA((8,)), DMA((8,)),
        ],
        0,
        kv_sent.reshape(4, token_rows // 4, 640), places_sent, w_sent, output_cotangent,
        fqn, fqr, own_positions[:, None], cosine, sine, query_latent_rows, query_adapter_first,
        qbn, qbr, output_adapter_first, output_adapter_second, latent_up_weight,
    )

    part = jnp.concatenate([o_part, q_part, jnp.zeros((token_rows, 128 - 2 * rank), jnp.float32)], -1)
    rows = token_rows // 8
    low = call(
        head_kernel, shaped((8, rows, 128)),
        [
            VMEM((7, rows, 128), jnp.float32), VMEM((rows, 128), jnp.bfloat16),
            DMA((7,)), DMA((7,)), DMA((7,)), DMA((7,)),
        ],
        2, part.reshape(8, rows, 128),
    ).reshape(token_rows, 128)
    output_rank_rows = low[:, :rank]
    query_adapter_gradient = low[:, rank:2 * rank]

    qa_term = contract_rows(query_adapter_gradient, query_latent_rows)
    ob_term = contract_rows(output_rank_rows, output_cotangent)
    ob_term = ob_term.astype(jnp.bfloat16).reshape(rank, 8, 4, 2, held_columns)
    ob_term = ob_term.transpose(3, 2, 1, 0, 4).reshape(64, -1, 128)
    lead = [term.astype(jnp.bfloat16).reshape(64, -1, 128) for term in (qbn_term, qbr_term, oa_term, qa_term)]
    sizes = [term.shape[1] for term in lead]
    pieces = jnp.concatenate(lead + [ob_term], 1)
    pieces = jnp.pad(pieces, ((0, 0), (0, 32 - pieces.shape[1]), (0, 0)))
    full, tail = call(
        reduce_kernel,
        (shaped((2, 4, 8, 16, 128)), shaped((16, 128), jnp.float32)),
        [
            VMEM((4, 8, 32, 128), bf), VMEM((4, 8, 32, 128), bf), VMEM((3, 8, 32, 128), bf),
            VMEM((8, 32, 128), bf), VMEM((7, 32, 128), bf), VMEM((16, 128), bf),
            VMEM((8, 16, 128), bf), VMEM((4, 8, 16, 128), bf), DMA((22,)), DMA((22,)), DMA((2,)),
        ],
        3, pieces.reshape(2, 4, 8, 32, 128),
    )
    full = full.reshape(64, 16, 128).astype(jnp.float32)
    ends = [sum(sizes[: i + 1]) for i in range(4)]
    grad_qb = jnp.concatenate(
        [
            full[:, :ends[0]].reshape(rank, head_number, PLAIN_WIDTH),
            full[:, ends[0]:ends[1]].reshape(rank, head_number, ROTARY_WIDTH),
        ],
        -1,
    ).reshape(rank, -1)
    grad_oa = full[:, ends[1]:ends[2]].reshape(oa_term.shape).T
    grad_qa = full[:, ends[2]:].reshape(qa_term.shape).T
    grad_ob = tail[:ob_term.shape[1]].reshape(rank, held_columns)
    return (grad_qa, grad_qb, grad_oa, grad_ob)


def solution(mesh):
    return jax.shard_map(
        body,
        mesh=mesh,
        in_specs=(
            P("ctx", "head"),
            P("ctx", None),
            P("ctx", None),
            P("ctx", None),
            P(None, "head"),
            P(),
            P(None, "head"),
            P("head", None),
            P(),
            P("head", "ctx"),
            P("ctx", None),
        ),
        out_specs=(P(), P(None, "head"), P("head", None), P(None, "ctx")),
        check_vma=False,
    )
```

```python
import functools

import jax
import jax.numpy as jnp
from jax import lax
from jax.experimental import pallas as pl
from jax.experimental.pallas import tpu as pltpu
from jax.sharding import PartitionSpec as P

PLAIN_WIDTH = 128
ROTARY_WIDTH = 64
VALUE_WIDTH = 128
KVL = 512
SPAN = 8
ROPE_BASE = 10000.0
MESH = pl.DeviceIdType.MESH
VMEM = pltpu.VMEM
DMA = pltpu.SemaphoreType.DMA


def block_positions(offsets, half_rows):
    steps = jnp.arange(half_rows, dtype=jnp.int32)
    return jnp.concatenate([offsets[..., :1] + steps, offsets[..., 1:] + steps], -1)


def columns_contract(left, right):
    return lax.dot_general(
        left, right, (((1,), (1,)), ((), ())), preferred_element_type=jnp.float32
    )


def send(src, dst, send_sem, recv_sem, axis, target):
    copy = pltpu.make_async_remote_copy(
        src_ref=src,
        dst_ref=dst,
        send_sem=send_sem,
        recv_sem=recv_sem,
        device_id={axis: target},
        device_id_type=MESH,
    )
    copy.start()
    return copy


def places(place):
    core = lax.rem(place, 2)
    y = lax.rem(place // 2, 8)
    z = place // 16
    partner = place + 1 - 2 * core
    return core, y, z, partner


def dot(left, right):
    return jnp.dot(left, right, preferred_element_type=jnp.float32)


def turned(vectors, cosine, sine):
    lane = lax.broadcasted_iota(jnp.int32, vectors.shape, 1)
    other = jnp.where(
        lax.rem(lane, 64) < 32, pltpu.roll(vectors, 96, 1), pltpu.roll(vectors, 32, 1)
    )
    return vectors * cosine + other * sine


def tree_reduce(
    at, x, r1, t1, r2, t2, r3, g0, ga, gy, full, tail, send_sem, recv_sem, local_sem, sent
):
    core, row, slot, partner, near, near_at, kin, kin_at = at
    used, kept = x.shape[2], gy.shape[1]

    def go(index, src, dst, target):
        copy = send(src, dst, send_sem.at[index], recv_sem.at[index], "ctx", target)
        sent.append(copy)
        return copy

    copy = go(0, x.at[1 - core], r1, partner)
    yield
    copy.wait_recv()
    t1[...] = (x[core].astype(jnp.float32) + r1[...].astype(jnp.float32)).astype(jnp.bfloat16)
    copies = [go(1 + i, t1.at[near[i]], r2.at[i], near_at[i]) for i in range(3)]
    yield
    total = x[core, row].astype(jnp.float32) + r1[row].astype(jnp.float32)
    for i, copy in enumerate(copies):
        copy.wait_recv()
        total = total + r2[i].astype(jnp.float32)
    total = total.astype(jnp.bfloat16)
    blank = jnp.zeros(total.shape[1:], jnp.bfloat16)
    for i in range(8):
        t2[i, 0] = total[i] if i < kept else blank
        if tail is not None:
            first = kept + 2 * (i // 3)
            t2[i, 1] = total[first]
            t2[i, 2] = total[first + 1]
    copies = [go(4 + i, t2.at[kin[i]], r3.at[i], kin_at[i]) for i in range(7)]
    yield
    total = t2[slot].astype(jnp.float32)
    for i, copy in enumerate(copies):
        copy.wait_recv()
        total = total + r3[i].astype(jnp.float32)
    if tail is not None:
        tail(total[1:3].reshape(32, 128))
    lead = total[0].astype(jnp.bfloat16)
    g0[...] = lead
    ga[slot] = lead
    copies = [go(11 + i, g0, ga.at[slot], kin_at[i]) for i in range(7)]
    yield
    for copy in copies:
        copy.wait_recv()
    own = pltpu.make_async_copy(ga.at[pl.ds(0, kept)], gy.at[row], local_sem.at[0])
    own.start()
    copies = [go(18 + i, ga.at[pl.ds(0, kept)], gy.at[row], near_at[i]) for i in range(3)]
    yield
    for copy in copies:
        copy.wait_recv()
    own.wait()
    last = pltpu.make_async_copy(gy, full.at[core], local_sem.at[1])
    last.start()
    copy = go(21, gy, full.at[core], partner)
    yield
    copy.wait_recv()
    last.wait()
    yield


def attend_kernel(
    kv_ref, places_ref, own_pos_ref, cos_ref, sin_ref,
    w_ref, cot_ref, fq_ref, ql_ref, qa_ref, qb_ref, oa_ref, ob_ref, up_ref,
    qa_out, qb_out, oa_out, ob_out,
    kv_all, place_all, w_all, cot_all, d_mine, d_all,
    fq_s, ql_s, qa_s, qb_s, oa_s, ob_s, up_s,
    qn_s, qr_s, kcat_s, val_s, wt_s, att_s, grad_s,
    part_s, hx_s, hy_s, hz_s,
    x1, r11, t11, r12, t12, r13, g10, ga1, gy1, full1,
    x2, r21, t21, r22, t22, r23, g20, ga2, gy2, full2,
    local_sem, kv_s, kv_r, st_s, st_r, pair_s, pair_r, z_s, z_r, y_s, y_r, x_s, x_r, f_s, f_r,
    h_s, h_r, tree_s, tree_r, tree_local,
):
    place = lax.axis_index("ctx")
    core, y, z, partner = places(place)
    slot = place // 8
    head = lax.axis_index("head")
    x, block = lax.rem(head, 4), (head // 4) * 4
    right, left = block + lax.rem(x + 1, 4), block + lax.rem(x + 3, 4)
    kin = [lax.rem(place + 8 * step, 64) for step in range(1, SPAN)]
    up = z * 16 + lax.rem(y + 1, 8) * 2 + core
    down = z * 16 + lax.rem(y + 7, 8) * 2 + core
    row = lax.rem(y, 4)
    kin_slot = [lax.rem(slot + step, 8) for step in range(1, 8)]
    near = [lax.rem(row + step, 4) for step in range(1, 4)]
    near_at = [8 * slot + 2 * other + core for other in near]
    beside = [block + lax.rem(x + step, 4) for step in range(1, 4)]
    facing = 4 - block + x
    barrier = pltpu.get_barrier_semaphore()
    for target in kin + near_at + [partner, up, down]:
        pl.semaphore_signal(barrier, inc=1, device_id={"ctx": target}, device_id_type=MESH)
    for target in beside + [facing]:
        pl.semaphore_signal(barrier, inc=1, device_id={"head": target}, device_id_type=MESH)
    pl.semaphore_wait(barrier, len(kin) + len(near_at) + 7)
    mine = pl.ds(pl.multiple_of(core * 512, 512), 512)
    theirs = pl.ds(pl.multiple_of((1 - core) * 512, 512), 512)

    own = [
        pltpu.make_async_copy(kv_ref.at[x], kv_all.at[slot, x], local_sem.at[0]),
        pltpu.make_async_copy(places_ref, place_all.at[slot], local_sem.at[1]),
        pltpu.make_async_copy(w_ref.at[:, mine], w_all.at[z, y, core], local_sem.at[2]),
        pltpu.make_async_copy(cot_ref, cot_all.at[core], local_sem.at[3]),
    ]
    for copy in own:
        copy.start()
    pending = []
    swap_w = send(
        w_ref.at[:, theirs], w_all.at[z, y, core], pair_s.at[0], pair_r.at[0], "ctx", partner
    )
    first = []
    for step in range(1, SPAN):
        i = step - 1
        first.append(send(kv_ref.at[x], kv_all.at[slot, x], kv_s.at[i], kv_r.at[i], "ctx", kin[i]))
    for i in range(SPAN - 1):
        pending.append(
            send(places_ref, place_all.at[slot], st_s.at[i], st_r.at[i], "ctx", kin[i])
        )
    swap_cot = send(cot_ref, cot_all.at[core], pair_s.at[1], pair_r.at[1], "ctx", partner)
    pending.append(swap_cot)
    across = [
        [
            send(kv_ref.at[x], kv_all.at[slot, x], x_s.at[side, 0], x_r.at[side, 0], "head", target)
        ]
        for side, target in ((0, right), (1, left))
    ]
    line = []
    for step in range(1, 4):
        target = lax.rem(z + step, 4) * 16 + y * 2 + core
        line.append([
            send(
                w_ref.at[:, mine], w_all.at[z, y, core],
                z_s.at[step - 1, 0], z_r.at[step - 1, 0], "ctx", target,
            )
        ])

    loads = [
        pltpu.make_async_copy(src, dst, local_sem.at[5 + i])
        for i, (src, dst) in enumerate((
            (ql_ref, ql_s), (qa_ref, qa_s), (fq_ref, fq_s), (qb_ref, qb_s), (up_ref, up_s),
            (oa_ref, oa_s), (ob_ref, ob_s),
        ))
    ]
    for copy in loads:
        copy.start()
    for copy in loads[:4]:
        copy.wait()
    low = columns_contract(ql_s[...], qa_s[...]).astype(jnp.bfloat16)
    low_turned = columns_contract(qa_s[...], ql_s[...]).astype(jnp.bfloat16)
    early = lax.broadcasted_iota(jnp.int32, (low.shape[0], 128), 1) < 64
    for pair in range(4):
        lanes = slice(384 * pair, 384 * pair + 384)
        vectors = fq_s[:, lanes].astype(jnp.float32) + dot(low, qb_s[:, lanes])
        one, two, three = [vectors[:, 128 * i:128 * i + 128] for i in range(3)]
        qn_s[:, 256 * pair:256 * pair + 128] = one.astype(jnp.bfloat16)
        qn_s[:, 256 * pair + 128:256 * pair + 256] = jnp.where(
            early, pltpu.roll(two, 64, 1), pltpu.roll(three, 64, 1)
        ).astype(jnp.bfloat16)
        qr_s[:, 128 * pair:128 * pair + 128] = turned(
            jnp.where(early, two, three), cos_ref[...], sin_ref[...]
        ).astype(jnp.bfloat16)

    swap_w.wait_recv()
    for step in range(1, 4):
        target = lax.rem(z + step, 4) * 16 + y * 2 + core
        line[step - 1].append(
            send(
                w_all.at[z, y, 1 - core], w_all.at[z, y, 1 - core],
                z_s.at[step - 1, 1], z_r.at[step - 1, 1], "ctx", target,
            )
        )
    own[2].wait()
    rings = {}

    def ring(step, unit):
        depth = lax.rem(z - unit + 4, 4)
        if step == 1 and unit:
            line[unit - 1][0].wait_recv()
            line[unit - 1][1].wait_recv()
        for side, target in ((0, up), (1, down)):
            if step > 1 and (side, step - 1, unit) in rings:
                rings[side, step - 1, unit].wait_recv()
            if step == 5 or (step == 4 and (unit // 2) != side):
                continue
            shift = -(step - 1) if side == 0 else step - 1
            column = lax.rem(y + shift + 8, 8)
            rings[side, step, unit] = send(
                w_all.at[depth, column], w_all.at[depth, column],
                y_s.at[side, step - 1, unit], y_r.at[side, step - 1, unit], "ctx", target,
            )

    ring(1, 0)
    for i in range(SPAN - 1):
        first[i].wait_recv()
        source = lax.rem(slot + 7 - i, 8)
        for side, target in ((0, right), (1, left)):
            across[side].append(
                send(
                    kv_all.at[source, x], kv_all.at[source, x],
                    x_s.at[side, i + 1], x_r.at[side, i + 1], "head", target,
                )
            )
    for unit in range(1, 4):
        ring(1, unit)
    relays = []
    for i in range(SPAN):
        source = lax.rem(slot + 8 - i, 8)
        across[0][i].wait_recv()
        across[1][i].wait_recv()
        if i % 2 == 0:
            target, lane = right, lax.rem(x + 3, 4)
        else:
            target, lane = left, lax.rem(x + 1, 4)
        relays.append(
            send(
                kv_all.at[source, lane], kv_all.at[source, lane],
                f_s.at[i], f_r.at[i], "head", target,
            )
        )
    for unit in range(4):
        ring(2, unit)
    own[0].wait()
    own[1].wait()
    for copy in relays + pending[:SPAN - 1]:
        copy.wait_recv()

    for copy in loads[4:]:
        copy.wait()
    positions = jnp.concatenate([place_all[i, 0:1, :] for i in range(SPAN)], 1)
    keys = positions.shape[1]
    visible = positions <= own_pos_ref[...]
    latents = kv_all[...].reshape(keys, 640)
    rope2 = latents[:, KVL:]
    scale = (PLAIN_WIDTH + ROTARY_WIDTH) ** (-0.5)
    lane_half = lax.broadcasted_iota(jnp.int32, (qr_s.shape[0], 128), 1) // 64

    def forward(number, total):
        kv = dot(latents[:, :KVL], up_s[:, pl.ds(pl.multiple_of(number * 256, 256), 256)])
        kv = kv.astype(jnp.bfloat16)
        kcat_s[number, :, :128] = kv[:, :128]
        kcat_s[number, :, 128:] = rope2
        val_s[number] = kv[:, 128:]
        plain = qn_s[:, pl.ds(pl.multiple_of(number * 128, 128), 128)]
        turn = qr_s[:, pl.ds(pl.multiple_of((number // 2) * 128, 128), 128)].astype(jnp.float32)
        turn = jnp.where(lane_half == lax.rem(number, 2), turn, 0.0).astype(jnp.bfloat16)
        query = jnp.concatenate([plain, turn], 1)
        scores = columns_contract(query, kcat_s[number]) * scale
        scores = jnp.where(visible, scores, -jnp.inf)
        expo = jnp.exp(scores - jnp.max(scores, -1, keepdims=True))
        weights = (expo / jnp.sum(expo, -1, keepdims=True)).astype(jnp.bfloat16)
        wt_s[number] = weights
        attended = dot(weights, val_s[number]).astype(jnp.bfloat16)
        att_s[:, pl.ds(pl.multiple_of(number * 128, 128), 128)] = attended
        return total + columns_contract(
            oa_s[:, pl.ds(pl.multiple_of(number * 128, 128), 128)], attended
        )

    total = jnp.zeros((32, 128), jnp.float32)
    for part in range(4):
        total = lax.fori_loop(2 * part, 2 * part + 2, forward, total)
        if part < 3:
            for unit in range(4):
                ring(part + 3, unit)
    part_s[:32] = total
    swap_cot.wait_recv()
    own[3].wait()

    tokens, half_out = d_mine.shape[1], d_mine.shape[2]
    cot = cot_all[...].reshape(2 * tokens, cot_all.shape[2])
    rank = columns_contract(cot, ob_s[...]).astype(jnp.bfloat16)
    d_half = dot(cot, w_all[...].reshape(cot.shape[1], half_out)) + dot(rank, oa_s[:, mine])
    d_mine[...] = d_half.astype(jnp.bfloat16).reshape(d_mine.shape)
    swap_d = send(
        d_mine.at[1 - core], d_all.at[core], pair_s.at[2], pair_r.at[2], "ctx", partner
    )
    keep = pltpu.make_async_copy(d_mine.at[core], d_all.at[core], local_sem.at[4])
    keep.start()
    rank_turned = columns_contract(ob_s[...], cot_all[core]).astype(jnp.bfloat16)
    oa_term = dot(rank_turned, att_s[...]).astype(jnp.bfloat16)
    for unit in range(24, 40):
        high, tile = (unit - 24) // 8, (unit - 24) % 8
        x1[unit // 20, unit // 5 % 4, unit % 5] = oa_term[
            16 * high:16 * high + 16, 128 * tile:128 * tile + 128
        ]
    swap_d.wait_recv()
    keep.wait()

    def backward(pair, total):
        turns, plains = [], []
        for even in range(2):
            number = 2 * pair + even
            lanes = pl.ds(pl.multiple_of(lax.rem(number, 4) * 128, 128), 128)
            d_prob = columns_contract(d_all[number // 4, :, lanes], val_s[number])
            weights = wt_s[number].astype(jnp.float32)
            delta = jnp.sum(weights * d_prob, -1, keepdims=True)
            d_score = (weights * (d_prob - delta) * scale).astype(jnp.bfloat16)
            grad = dot(d_score, kcat_s[number])
            plains.append(grad[:, :128])
            turns.append(turned(grad[:, 128:], cos_ref[...], -sin_ref[...]))
        turn = jnp.where(early, turns[0], turns[1])
        moved = pltpu.roll(plains[1], 64, 1)
        parts = [plains[0], jnp.where(early, turn, moved), jnp.where(early, moved, turn)]
        for i, piece in enumerate(parts):
            at = pl.ds(pl.multiple_of(pair * 384 + i * 128, 128), 128)
            piece = piece.astype(jnp.bfloat16)
            grad_s[:, at] = piece
            total = total + columns_contract(qb_s[:, at], piece)
        return total

    part_s[32:] = lax.fori_loop(0, 4, backward, jnp.zeros((32, 128), jnp.float32))
    heads = []
    for i in range(3):
        heads.append(send(part_s, hx_s.at[x], h_s.at[i], h_r.at[i], "head", beside[i]))
    hx_s[x] = part_s[...]
    qb_term = dot(low_turned, grad_s[...]).astype(jnp.bfloat16)
    for unit in range(24):
        high, tile = unit // 12, unit % 12
        x1[unit // 20, unit // 5 % 4, unit % 5] = qb_term[
            16 * high:16 * high + 16, 128 * tile:128 * tile + 128
        ]
    at = (core, row, slot, partner, near, near_at, kin_slot, kin)
    sent = []
    wide = tree_reduce(
        at, x1, r11, t11, r12, t12, r13, g10, ga1, gy1, full1, None,
        tree_s.at[0], tree_r.at[0], tree_local.at[0], sent,
    )
    next(wide)
    for copy in heads:
        copy.wait_recv()
    hy_s[...] = hx_s[0] + hx_s[1] + hx_s[2] + hx_s[3]
    heads.append(send(hy_s, hz_s, h_s.at[3], h_r.at[3], "head", facing))
    next(wide)
    heads[3].wait_recv()
    sums = (hy_s[...] + hz_s[...]).astype(jnp.bfloat16)
    qa_term = dot(sums[32:], ql_s[...]).astype(jnp.bfloat16)
    for unit in range(24):
        high, tile = unit // 12, unit % 12
        x2[unit // 12, unit // 3 % 4, unit % 3] = qa_term[
            16 * high:16 * high + 16, 128 * tile:128 * tile + 128
        ]
    ob_term = dot(sums[:32], cot_all[core])
    lane = lax.broadcasted_iota(jnp.int32, (32, 128), 1)

    def shifted(start, to):
        tile, offset = start // 128, start % 128
        shift = (to - offset) % 128
        value = pltpu.roll(ob_term[:, 128 * tile:128 * tile + 128], shift, 1)
        if offset + 40 > 128:
            after = pltpu.roll(ob_term[:, 128 * tile + 128:128 * tile + 256], shift, 1)
            value = jnp.where(lane < to + 128 - offset, value, after)
        return value

    for half in range(2):
        for line_row in range(4):
            for third in range(3):
                packed = jnp.zeros((32, 128), jnp.float32)
                for i in range(3):
                    member = 3 * third + i
                    if member > 7:
                        continue
                    value = shifted(40 * (8 * member + 2 * line_row + half), 40 * i)
                    inside = (lane >= 40 * i) & (lane < 40 * i + 40)
                    packed = jnp.where(inside, value, packed)
                packed = packed.astype(jnp.bfloat16)
                x2[half, line_row, 3 + 2 * third] = packed[:16]
                x2[half, line_row, 4 + 2 * third] = packed[16:]

    def tail(total):
        third = lax.rem(slot, 3)
        value = jnp.where(third == 1, pltpu.roll(total, 88, 1), total)
        value = jnp.where(third == 2, pltpu.roll(total, 48, 1), value)
        ob_out[...] = value[:, :40]

    slim = tree_reduce(
        at, x2, r21, t21, r22, t22, r23, g20, ga2, gy2, full2, tail,
        tree_s.at[1], tree_r.at[1], tree_local.at[1], sent,
    )
    for _ in range(5):
        next(slim)
        next(wide)
    for unit in range(40):
        value = full1[unit // 20, unit // 5 % 4, unit % 5].astype(jnp.float32)
        if unit < 24:
            high, tile, out = unit // 12, unit % 12, qb_out
        else:
            high, tile, out = (unit - 24) // 8, (unit - 24) % 8, oa_out
        out[16 * high:16 * high + 16, 128 * tile:128 * tile + 128] = value
    next(slim)
    next(slim)
    for unit in range(24):
        high, tile = unit // 12, unit % 12
        qa_out[16 * high:16 * high + 16, 128 * tile:128 * tile + 128] = full2[
            unit // 12, unit // 3 % 4, unit % 3
        ].astype(jnp.float32)

    done = first + pending + [swap_w, swap_d] + line[0] + line[1] + line[2] + heads + sent
    for copy in done + across[0] + across[1] + relays + list(rings.values()):
        copy.wait_send()


def shaped(shape, dtype=jnp.bfloat16):
    return jax.ShapeDtypeStruct(shape, dtype)


def body(
    frozen_queries,
    query_latent_rows,
    key_value_latent,
    block_starts,
    latent_up_weight,
    query_adapter_first,
    query_adapter_second,
    output_adapter_first,
    output_adapter_second,
    frozen_output_weight,
    output_cotangent,
):
    token_rows = frozen_queries.shape[0]
    half_rows = token_rows // 2
    per_head_width = PLAIN_WIDTH + ROTARY_WIDTH
    head_number = query_adapter_second.shape[1] // per_head_width
    width = output_cotangent.shape[1]
    rank = query_adapter_first.shape[1]
    held_rows, held_columns = frozen_output_weight.shape
    half_out = held_rows // 2
    bf = jnp.bfloat16
    own_positions = block_positions(block_starts[0], half_rows)

    lane = jnp.arange(128, dtype=jnp.int32)
    freq = ROPE_BASE ** (-(lane % 32).astype(jnp.float32) * 2.0 / ROTARY_WIDTH)
    angle = own_positions.astype(jnp.float32)[:, None] * freq[None, :]
    cosine = jnp.cos(angle)
    sine = jnp.where(lane[None, :] % 64 < 32, -jnp.sin(angle), jnp.sin(angle))
    raw = key_value_latent[:, KVL:].astype(jnp.float32)
    other = jnp.concatenate([raw[:, 32:], raw[:, :32]], 1)
    rope_key = (
        jnp.concatenate([raw, raw], 1) * cosine + jnp.concatenate([other, other], 1) * sine
    ).astype(bf)
    kv_sent = jnp.concatenate([key_value_latent[:, :KVL], rope_key], -1)
    places_sent = jnp.broadcast_to(own_positions[None, :], (8, token_rows))
    keys = SPAN * token_rows
    plain, turn = head_number * PLAIN_WIDTH, head_number * ROTARY_WIDTH

    def tree(used, kept, deep):
        return [
            VMEM((2, 4, used, 16, 128), bf), VMEM((4, used, 16, 128), bf),
            VMEM((4, used, 16, 128), bf), VMEM((3, used, 16, 128), bf),
            VMEM((8, deep, 16, 128), bf), VMEM((7, deep, 16, 128), bf), VMEM((16, 128), bf),
            VMEM((8, 16, 128), bf), VMEM((4, kept, 16, 128), bf), VMEM((2, 4, kept, 16, 128), bf),
        ]

    close, far = pl.BlockSpec(memory_space=VMEM), pl.BlockSpec(memory_space=pltpu.HBM)
    f32 = jnp.float32
    grad_qa, grad_qb, grad_oa, grad_ob = pl.pallas_call(
        attend_kernel,
        out_shape=(
            shaped((rank, query_latent_rows.shape[1]), f32),
            shaped(query_adapter_second.shape, f32),
            shaped((rank, held_rows), f32),
            shaped((rank, held_columns), f32),
        ),
        in_specs=[close] * 5 + [far] * 9,
        out_specs=(close,) * 4,
        scratch_shapes=[
            VMEM((SPAN, 4, token_rows // 4, 640), bf), VMEM((SPAN, 8, 128), jnp.int32),
            VMEM((4, 8, 2, held_columns, half_out), bf), VMEM((2, token_rows, width), bf),
            VMEM((2, token_rows, half_out), bf), VMEM((2, token_rows, half_out), bf),
            VMEM(frozen_queries.shape, bf), VMEM(query_latent_rows.shape, bf),
            VMEM((rank, query_latent_rows.shape[1]), bf), VMEM(query_adapter_second.shape, bf),
            VMEM((rank, held_rows), bf), VMEM((rank, width), bf), VMEM(latent_up_weight.shape, bf),
            VMEM((token_rows, plain), bf), VMEM((token_rows, turn), bf),
            VMEM((head_number, keys, 256), bf), VMEM((head_number, keys, 128), bf),
            VMEM((head_number, token_rows, keys), bf), VMEM((token_rows, held_rows), bf),
            VMEM(frozen_queries.shape, bf),
            VMEM((2 * rank, 128), f32), VMEM((4, 2 * rank, 128), f32),
            VMEM((2 * rank, 128), f32), VMEM((2 * rank, 128), f32),
            *tree(5, 5, 1), *tree(9, 3, 3),
            DMA((12,)), DMA((7,)), DMA((7,)), DMA((7,)), DMA((7,)), DMA((3,)), DMA((3,)),
            DMA((3, 2)), DMA((3, 2)), DMA((2, 4, 4)), DMA((2, 4, 4)), DMA((2, 8)), DMA((2, 8)),
            DMA((8,)), DMA((8,)), DMA((4,)), DMA((4,)), DMA((2, 22)), DMA((2, 22)), DMA((2, 2)),
        ],
        compiler_params=pltpu.CompilerParams(
            collective_id=0, has_side_effects=True, vmem_limit_bytes=56 * 1024 * 1024
        ),
    )(
        kv_sent.reshape(4, token_rows // 4, 640), places_sent, own_positions[:, None], cosine, sine,
        frozen_output_weight.T, output_cotangent, frozen_queries, query_latent_rows,
        query_adapter_first.T, query_adapter_second, output_adapter_first.T,
        output_adapter_second, latent_up_weight,
    )
    return (grad_qa.T, grad_qb, grad_oa.T, grad_ob)


def solution(mesh):
    return jax.shard_map(
        body,
        mesh=mesh,
        in_specs=(
            P("ctx", "head"),
            P("ctx", None),
            P("ctx", None),
            P("ctx", None),
            P(None, "head"),
            P(),
            P(None, "head"),
            P("head", None),
            P(),
            P("head", "ctx"),
            P("ctx", None),
        ),
        out_specs=(P(), P(None, "head"), P("head", None), P(None, "ctx")),
        check_vma=False,
    )
```

```python
import math

import jax
import jax.numpy as jnp
from jax import lax
from jax.experimental import pallas as pl
from jax.experimental.pallas import tpu as pltpu
from jax.sharding import PartitionSpec as P

PLAIN_WIDTH = 128
ROTARY_WIDTH = 64
VALUE_WIDTH = 128
KVL = 512
SPAN = 8
ROPE_BASE = 10000.0
MESH = pl.DeviceIdType.MESH
VMEM = pltpu.VMEM
DMA = pltpu.SemaphoreType.DMA


def columns_contract(left, right):
    return lax.dot_general(
        left, right, (((1,), (1,)), ((), ())), preferred_element_type=jnp.float32
    )


def send(src, dst, send_sem, recv_sem, axis, target):
    copy = pltpu.make_async_remote_copy(
        src_ref=src,
        dst_ref=dst,
        send_sem=send_sem,
        recv_sem=recv_sem,
        device_id={axis: target},
        device_id_type=MESH,
    )
    copy.start()
    return copy


def places(place):
    core = lax.rem(place, 2)
    y = lax.rem(place // 2, 8)
    z = place // 16
    partner = place + 1 - 2 * core
    return core, y, z, partner


def dot(left, right):
    return jnp.dot(left, right, preferred_element_type=jnp.float32)


def turned(vectors, cosine, sine):
    lane = lax.broadcasted_iota(jnp.int32, vectors.shape, 1)
    other = jnp.where(
        lax.rem(lane, 64) < 32, pltpu.roll(vectors, 96, 1), pltpu.roll(vectors, 32, 1)
    )
    return vectors * cosine + other * sine


def tree_reduce(at, x, r1, t1, r2, t2, r3, g0, full, tail, send_sem, recv_sem, local_sem, sent):
    core, row, slot, partner, near, near_at, kin, kin_at, group_at = at
    kept = full.shape[2]

    def go(index, src, dst, target):
        copy = send(src, dst, send_sem.at[index], recv_sem.at[index], "ctx", target)
        sent.append(copy)
        return copy

    copy = go(0, x.at[1 - core], r1, partner)
    yield
    copy.wait_recv()
    t1[...] = (x[core].astype(jnp.float32) + r1[...].astype(jnp.float32)).astype(jnp.bfloat16)
    copies = [go(1 + i, t1.at[near[i]], r2.at[i], near_at[i]) for i in range(3)]
    yield
    total = x[core, row].astype(jnp.float32) + r1[row].astype(jnp.float32)
    for i, copy in enumerate(copies):
        copy.wait_recv()
        total = total + r2[i].astype(jnp.float32)
    total = total.astype(jnp.bfloat16)
    for i in range(8):
        t2[i, :kept] = total[:kept]
        if tail is not None:
            first = kept + 2 * (i // 3)
            t2[i, kept:] = total[first:first + 2]
    copies = [go(4 + i, t2.at[kin[i]], r3.at[slot], kin_at[i]) for i in range(7)]
    r3[slot] = t2[slot]
    yield
    for copy in copies:
        copy.wait_recv()
    total = r3[0].astype(jnp.float32)
    for i in range(1, 8):
        total = total + r3[i].astype(jnp.float32)
    if tail is not None:
        tail(total[kept:].reshape(32, 128))
    lead = total[:kept].astype(jnp.bfloat16)
    g0[...] = lead
    full[core, row] = lead
    copies = [go(11 + i, g0, full.at[core, row], group_at[i]) for i in range(7)]
    yield
    for copy in copies:
        copy.wait_recv()
    yield


def attend_kernel(
    starts_ref, kvt_ref,
    w_ref, cot_ref, fq_ref, ql_ref, qa_ref, qb_ref, oa_ref, ob_ref, up_ref,
    full_e, full_b, full_a, ob_out,
    kvt_s, kv_pre, place_pre, kv_ref, places_ref, cos_ref, sin_ref,
    kv_all, place_all, w_all, cot_all, d_mine, d_all,
    fq_s, ql_s, qa_s, qb_s, oa_s, ob_s, up_s,
    qn_s, qr_s, kcat_s, val_s, wt_s, att_s, grad_s,
    part_s, hx_s, hy_s, hz_s, po_s, ox_s, oy_s, oz_s,
    xe, re1, te1, re2, te2, re3, ge, xb, rb1, tb1, rb2, tb2, rb3, gb,
    xa, ra1, ta1, ra2, ta2, ra3, gq,
    local_sem, kv_s, kv_r, st_s, st_r, pair_s, pair_r, z_s, z_r, y_s, y_r, x_s, x_r, f_s, f_r,
    h_s, h_r, tree_s, tree_r, load_sem,
):
    place = lax.axis_index("ctx")
    core, y, z, partner = places(place)
    slot = place // 8
    head = lax.axis_index("head")
    x, block = lax.rem(head, 4), (head // 4) * 4
    right, left = block + lax.rem(x + 1, 4), block + lax.rem(x + 3, 4)
    kin = [lax.rem(place + 8 * step, 64) for step in range(1, SPAN)]
    up = z * 16 + lax.rem(y + 1, 8) * 2 + core
    down = z * 16 + lax.rem(y + 7, 8) * 2 + core
    row = lax.rem(y, 4)
    kin_slot = [lax.rem(slot + step, 8) for step in range(1, 8)]
    near = [lax.rem(row + step, 4) for step in range(1, 4)]
    near_at = [8 * slot + 2 * other + core for other in near]
    group_at = [8 * slot + lax.rem(lax.rem(place, 8) + step, 8) for step in range(1, 8)]
    beside = [block + lax.rem(x + step, 4) for step in range(1, 4)]
    facing = 4 - block + x
    barrier = pltpu.get_barrier_semaphore()
    for target in kin + group_at + [up, down]:
        pl.semaphore_signal(barrier, inc=1, device_id={"ctx": target}, device_id_type=MESH)
    for target in beside + [facing]:
        pl.semaphore_signal(barrier, inc=1, device_id={"head": target}, device_id_type=MESH)
    loads = [
        pltpu.make_async_copy(src, dst, load_sem.at[i])
        for i, (src, dst) in enumerate((
            (kvt_ref, kvt_s), (ql_ref, ql_s), (qa_ref, qa_s), (fq_ref, fq_s), (qb_ref, qb_s),
            (up_ref, up_s), (oa_ref, oa_s), (ob_ref, ob_s),
        ))
    ]
    for copy in loads:
        copy.start()
    start, middle = starts_ref[0, 0], starts_ref[0, 1]

    def spread(shape, axis):
        step = lax.broadcasted_iota(jnp.int32, shape, axis)
        return jnp.where(step < 64, step + start, step - 64 + middle)

    lane = lax.broadcasted_iota(jnp.int32, (128, 128), 1)
    power = lax.rem(lane, 32).astype(jnp.float32) * (-2.0 * math.log(ROPE_BASE) / ROTARY_WIDTH)
    angle = spread((128, 128), 0).astype(jnp.float32) * jnp.exp(power)
    cos_ref[...] = jnp.cos(angle)
    sine = jnp.sin(angle)
    sin_ref[...] = jnp.where(lax.rem(lane, 64) < 32, -sine, sine)
    place_pre[...] = spread((8, 128), 1)
    loads[0].wait()
    raw = kvt_s[KVL:].astype(jnp.float32)
    rope = turned(jnp.concatenate([raw, raw], 0).T, cos_ref[...], sin_ref[...])
    latent = kvt_s[:KVL].astype(jnp.float32).T
    kv_pre[:, :, :KVL] = latent.astype(jnp.bfloat16).reshape(4, 32, KVL)
    kv_pre[:, :, KVL:] = rope.astype(jnp.bfloat16).reshape(4, 32, 128)
    bounce = [
        pltpu.make_async_copy(kv_pre, kv_ref, load_sem.at[8]),
        pltpu.make_async_copy(place_pre, places_ref, load_sem.at[9]),
    ]
    for copy in bounce:
        copy.start()
    for copy in bounce:
        copy.wait()
    pl.semaphore_wait(barrier, len(kin) + len(group_at) + 6)
    mine = pl.ds(pl.multiple_of(core * 512, 512), 512)
    theirs = pl.ds(pl.multiple_of((1 - core) * 512, 512), 512)

    own = [
        pltpu.make_async_copy(kv_ref.at[x], kv_all.at[slot, x], local_sem.at[0]),
        pltpu.make_async_copy(places_ref, place_all.at[slot], local_sem.at[1]),
        pltpu.make_async_copy(w_ref.at[:, mine], w_all.at[z, y, core], local_sem.at[2]),
        pltpu.make_async_copy(cot_ref, cot_all.at[core], local_sem.at[3]),
    ]
    for copy in own:
        copy.start()
    pending = []
    swap_w = send(
        w_ref.at[:, theirs], w_all.at[z, y, core], pair_s.at[0], pair_r.at[0], "ctx", partner
    )
    first = []
    for step in range(1, SPAN):
        i = step - 1
        first.append(send(kv_ref.at[x], kv_all.at[slot, x], kv_s.at[i], kv_r.at[i], "ctx", kin[i]))
    for i in range(SPAN - 1):
        pending.append(
            send(places_ref, place_all.at[slot], st_s.at[i], st_r.at[i], "ctx", kin[i])
        )
    swap_cot = send(cot_ref, cot_all.at[core], pair_s.at[1], pair_r.at[1], "ctx", partner)
    pending.append(swap_cot)
    across = [
        [
            send(kv_ref.at[x], kv_all.at[slot, x], x_s.at[side, 0], x_r.at[side, 0], "head", target)
        ]
        for side, target in ((0, right), (1, left))
    ]
    line = []
    for step in range(1, 4):
        target = lax.rem(z + step, 4) * 16 + y * 2 + core
        line.append([
            send(
                w_ref.at[:, mine], w_all.at[z, y, core],
                z_s.at[step - 1, 0], z_r.at[step - 1, 0], "ctx", target,
            )
        ])

    for copy in loads[1:5]:
        copy.wait()
    low = columns_contract(ql_s[...], qa_s[...]).astype(jnp.bfloat16)
    low_turned = columns_contract(qa_s[...], ql_s[...]).astype(jnp.bfloat16)
    early = lax.broadcasted_iota(jnp.int32, (low.shape[0], 128), 1) < 64
    for pair in range(4):
        lanes = slice(384 * pair, 384 * pair + 384)
        vectors = fq_s[:, lanes].astype(jnp.float32) + dot(low, qb_s[:, lanes])
        one, two, three = [vectors[:, 128 * i:128 * i + 128] for i in range(3)]
        qn_s[:, 256 * pair:256 * pair + 128] = one.astype(jnp.bfloat16)
        qn_s[:, 256 * pair + 128:256 * pair + 256] = jnp.where(
            early, pltpu.roll(two, 64, 1), pltpu.roll(three, 64, 1)
        ).astype(jnp.bfloat16)
        qr_s[:, 128 * pair:128 * pair + 128] = turned(
            jnp.where(early, two, three), cos_ref[...], sin_ref[...]
        ).astype(jnp.bfloat16)

    swap_w.wait_recv()
    for step in range(1, 4):
        target = lax.rem(z + step, 4) * 16 + y * 2 + core
        line[step - 1].append(
            send(
                w_all.at[z, y, 1 - core], w_all.at[z, y, 1 - core],
                z_s.at[step - 1, 1], z_r.at[step - 1, 1], "ctx", target,
            )
        )
    own[2].wait()
    rings = {}

    def ring(step, unit):
        depth = lax.rem(z - unit + 4, 4)
        if step == 1 and unit:
            line[unit - 1][0].wait_recv()
            line[unit - 1][1].wait_recv()
        for side, target in ((0, up), (1, down)):
            if step > 1 and (side, step - 1, unit) in rings:
                rings[side, step - 1, unit].wait_recv()
            if step == 5 or (step == 4 and (unit // 2) != side):
                continue
            shift = -(step - 1) if side == 0 else step - 1
            column = lax.rem(y + shift + 8, 8)
            rings[side, step, unit] = send(
                w_all.at[depth, column], w_all.at[depth, column],
                y_s.at[side, step - 1, unit], y_r.at[side, step - 1, unit], "ctx", target,
            )

    ring(1, 0)
    for i in range(SPAN - 1):
        first[i].wait_recv()
        source = lax.rem(slot + 7 - i, 8)
        for side, target in ((0, right), (1, left)):
            across[side].append(
                send(
                    kv_all.at[source, x], kv_all.at[source, x],
                    x_s.at[side, i + 1], x_r.at[side, i + 1], "head", target,
                )
            )
    for unit in range(1, 4):
        ring(1, unit)
    relays = []
    for i in range(SPAN):
        source = lax.rem(slot + 8 - i, 8)
        across[0][i].wait_recv()
        across[1][i].wait_recv()
        if i % 2 == 0:
            target, lane = right, lax.rem(x + 3, 4)
        else:
            target, lane = left, lax.rem(x + 1, 4)
        relays.append(
            send(
                kv_all.at[source, lane], kv_all.at[source, lane],
                f_s.at[i], f_r.at[i], "head", target,
            )
        )
    for unit in range(4):
        ring(2, unit)
    own[0].wait()
    own[1].wait()
    for copy in relays + pending[:SPAN - 1]:
        copy.wait_recv()

    for copy in loads[5:]:
        copy.wait()
    positions = jnp.concatenate([place_all[i, 0:1, :] for i in range(SPAN)], 1)
    keys = positions.shape[1]
    visible = positions <= spread((128, 1), 0)
    latents = kv_all[...].reshape(keys, 640)
    rope2 = latents[:, KVL:]
    scale = (PLAIN_WIDTH + ROTARY_WIDTH) ** (-0.5)
    lane_half = lax.broadcasted_iota(jnp.int32, (qr_s.shape[0], 128), 1) // 64

    def forward(number, total):
        kv = dot(latents[:, :KVL], up_s[:, pl.ds(pl.multiple_of(number * 256, 256), 256)])
        kv = kv.astype(jnp.bfloat16)
        kcat_s[number, :, :128] = kv[:, :128]
        kcat_s[number, :, 128:] = rope2
        val_s[number] = kv[:, 128:]
        plain = qn_s[:, pl.ds(pl.multiple_of(number * 128, 128), 128)]
        turn = qr_s[:, pl.ds(pl.multiple_of((number // 2) * 128, 128), 128)].astype(jnp.float32)
        turn = jnp.where(lane_half == lax.rem(number, 2), turn, 0.0).astype(jnp.bfloat16)
        query = jnp.concatenate([plain, turn], 1)
        scores = columns_contract(query, kcat_s[number]) * scale
        scores = jnp.where(visible, scores, -jnp.inf)
        expo = jnp.exp(scores - jnp.max(scores, -1, keepdims=True))
        weights = (expo / jnp.sum(expo, -1, keepdims=True)).astype(jnp.bfloat16)
        wt_s[number] = weights
        attended = dot(weights, val_s[number]).astype(jnp.bfloat16)
        att_s[:, pl.ds(pl.multiple_of(number * 128, 128), 128)] = attended
        return total + columns_contract(
            oa_s[:, pl.ds(pl.multiple_of(number * 128, 128), 128)], attended
        )

    total = jnp.zeros((32, 128), jnp.float32)
    for part in range(4):
        total = lax.fori_loop(2 * part, 2 * part + 2, forward, total)
        if part < 3:
            for unit in range(4):
                ring(part + 3, unit)
    po_s[...] = total
    ox_s[x] = total
    heads = [send(po_s, ox_s.at[x], h_s.at[i], h_r.at[i], "head", beside[i]) for i in range(3)]
    swap_cot.wait_recv()
    own[3].wait()

    tokens, half_out = d_mine.shape[1], d_mine.shape[2]
    cot = cot_all[...].reshape(2 * tokens, cot_all.shape[2])
    rank = columns_contract(cot, ob_s[...]).astype(jnp.bfloat16)
    d_half = dot(cot, w_all[...].reshape(cot.shape[1], half_out)) + dot(rank, oa_s[:, mine])
    d_mine[...] = d_half.astype(jnp.bfloat16).reshape(d_mine.shape)
    swap_d = send(
        d_mine.at[1 - core], d_all.at[core], pair_s.at[2], pair_r.at[2], "ctx", partner
    )
    keep = pltpu.make_async_copy(d_mine.at[core], d_all.at[core], local_sem.at[4])
    keep.start()
    rank_turned = columns_contract(ob_s[...], cot_all[core]).astype(jnp.bfloat16)
    oa_term = dot(rank_turned, att_s[...]).astype(jnp.bfloat16)
    for unit in range(16):
        high, tile = unit // 8, unit % 8
        xe[unit // 8, unit // 2 % 4, unit % 2] = oa_term[
            16 * high:16 * high + 16, 128 * tile:128 * tile + 128
        ]
    for copy in heads:
        copy.wait_recv()
    oy_s[...] = ox_s[0] + ox_s[1] + ox_s[2] + ox_s[3]
    heads.append(send(oy_s, oz_s, h_s.at[3], h_r.at[3], "head", facing))
    swap_d.wait_recv()
    keep.wait()
    at = (core, row, slot, partner, near, near_at, kin_slot, kin, group_at)
    sent = []

    def backward(pair, total):
        turns, plains = [], []
        for even in range(2):
            number = 2 * pair + even
            lanes = pl.ds(pl.multiple_of(lax.rem(number, 4) * 128, 128), 128)
            d_prob = columns_contract(d_all[number // 4, :, lanes], val_s[number])
            weights = wt_s[number].astype(jnp.float32)
            delta = jnp.sum(weights * d_prob, -1, keepdims=True)
            d_score = (weights * (d_prob - delta) * scale).astype(jnp.bfloat16)
            grad = dot(d_score, kcat_s[number])
            plains.append(grad[:, :128])
            turns.append(turned(grad[:, 128:], cos_ref[...], -sin_ref[...]))
        turn = jnp.where(early, turns[0], turns[1])
        moved = pltpu.roll(plains[1], 64, 1)
        parts = [plains[0], jnp.where(early, turn, moved), jnp.where(early, moved, turn)]
        for i, piece in enumerate(parts):
            at = pl.ds(pl.multiple_of(pair * 384 + i * 128, 128), 128)
            piece = piece.astype(jnp.bfloat16)
            grad_s[:, at] = piece
            total = total + columns_contract(qb_s[:, at], piece)
        return total

    total = lax.fori_loop(0, 2, backward, jnp.zeros((32, 128), jnp.float32))
    heads[3].wait_recv()
    o_low = (oy_s[...] + oz_s[...]).astype(jnp.bfloat16)
    ob_term = dot(o_low, cot_all[core])
    lane = lax.broadcasted_iota(jnp.int32, (32, 128), 1)

    def shifted(start, to):
        tile, offset = start // 128, start % 128
        shift = (to - offset) % 128
        value = pltpu.roll(ob_term[:, 128 * tile:128 * tile + 128], shift, 1)
        if offset + 40 > 128:
            after = pltpu.roll(ob_term[:, 128 * tile + 128:128 * tile + 256], shift, 1)
            value = jnp.where(lane < to + 128 - offset, value, after)
        return value

    for half in range(2):
        for line_row in range(4):
            for third in range(3):
                packed = jnp.zeros((32, 128), jnp.float32)
                for i in range(3):
                    member = 3 * third + i
                    if member > 7:
                        continue
                    value = shifted(40 * (8 * member + 2 * line_row + half), 40 * i)
                    inside = (lane >= 40 * i) & (lane < 40 * i + 40)
                    packed = jnp.where(inside, value, packed)
                packed = packed.astype(jnp.bfloat16)
                xe[half, line_row, 2 + 2 * third] = packed[:16]
                xe[half, line_row, 3 + 2 * third] = packed[16:]

    def tail(total):
        third = lax.rem(slot, 3)
        value = jnp.where(third == 1, pltpu.roll(total, 88, 1), total)
        value = jnp.where(third == 2, pltpu.roll(total, 48, 1), value)
        ob_out[...] = value

    soon = tree_reduce(
        at, xe, re1, te1, re2, te2, re3, ge, full_e, tail,
        tree_s.at[0], tree_r.at[0], None, sent,
    )
    next(soon)
    total = lax.fori_loop(2, 3, backward, total)
    next(soon)
    total = lax.fori_loop(3, 4, backward, total)
    part_s[...] = total
    hx_s[x] = total
    next(soon)
    late = [send(part_s, hx_s.at[x], h_s.at[4 + i], h_r.at[4 + i], "head", beside[i]) for i in range(3)]
    qb_term = dot(low_turned, grad_s[...]).astype(jnp.bfloat16)
    for unit in range(24):
        high, tile = unit // 12, unit % 12
        xb[unit // 12, unit // 3 % 4, unit % 3] = qb_term[
            16 * high:16 * high + 16, 128 * tile:128 * tile + 128
        ]
    wide = tree_reduce(
        at, xb, rb1, tb1, rb2, tb2, rb3, gb, full_b, None,
        tree_s.at[1], tree_r.at[1], None, sent,
    )
    next(wide)
    for copy in late:
        copy.wait_recv()
    hy_s[...] = hx_s[0] + hx_s[1] + hx_s[2] + hx_s[3]
    late.append(send(hy_s, hz_s, h_s.at[7], h_r.at[7], "head", facing))
    next(wide)
    next(soon)
    late[3].wait_recv()
    sums = (hy_s[...] + hz_s[...]).astype(jnp.bfloat16)
    qa_term = dot(sums, ql_s[...]).astype(jnp.bfloat16)
    for unit in range(24):
        high, tile = unit // 12, unit % 12
        xa[unit // 12, unit // 3 % 4, unit % 3] = qa_term[
            16 * high:16 * high + 16, 128 * tile:128 * tile + 128
        ]
    slim = tree_reduce(
        at, xa, ra1, ta1, ra2, ta2, ra3, gq, full_a, None,
        tree_s.at[2], tree_r.at[2], None, sent,
    )
    next(slim)
    next(slim)
    next(wide)
    next(slim)
    next(wide)
    next(soon)
    next(slim)
    next(wide)
    next(slim)
    heads += late

    done = first + pending + [swap_w, swap_d] + line[0] + line[1] + line[2] + heads + sent
    for copy in done + across[0] + across[1] + relays + list(rings.values()):
        copy.wait_send()


def finish_kernel(full_e, full_b, full_a, tail_ref, qa_out, qb_out, oa_out, ob_out):
    for source, out, kept in ((full_a, qa_out, 3), (full_b, qb_out, 3), (full_e, oa_out, 2)):
        tiles = out.shape[1] // 128
        for unit in range(8 * kept):
            high, tile = unit // tiles, unit % tiles
            out[16 * high:16 * high + 16, 128 * tile:128 * tile + 128] = source[
                unit // (4 * kept), unit // kept % 4, unit % kept
            ].astype(jnp.float32)
    ob_out[...] = tail_ref[...][:, :40]


def shaped(shape, dtype=jnp.bfloat16):
    return jax.ShapeDtypeStruct(shape, dtype)


def body(
    frozen_queries,
    query_latent_rows,
    key_value_latent,
    block_starts,
    latent_up_weight,
    query_adapter_first,
    query_adapter_second,
    output_adapter_first,
    output_adapter_second,
    frozen_output_weight,
    output_cotangent,
):
    token_rows = frozen_queries.shape[0]
    per_head_width = PLAIN_WIDTH + ROTARY_WIDTH
    head_number = query_adapter_second.shape[1] // per_head_width
    width = output_cotangent.shape[1]
    rank = query_adapter_first.shape[1]
    held_rows, held_columns = frozen_output_weight.shape
    half_out = held_rows // 2
    bf = jnp.bfloat16
    keys = SPAN * token_rows
    plain, turn = head_number * PLAIN_WIDTH, head_number * ROTARY_WIDTH

    def tree(used, kept, deep):
        return [
            VMEM((2, 4, used, 16, 128), bf), VMEM((4, used, 16, 128), bf),
            VMEM((4, used, 16, 128), bf), VMEM((3, used, 16, 128), bf),
            VMEM((8, deep, 16, 128), bf), VMEM((8, deep, 16, 128), bf), VMEM((kept, 16, 128), bf),
        ]

    close, far = pl.BlockSpec(memory_space=VMEM), pl.BlockSpec(memory_space=pltpu.HBM)
    f32 = jnp.float32
    pieces = pl.pallas_call(
        attend_kernel,
        out_shape=(
            shaped((2, 4, 2, 16, 128)),
            shaped((2, 4, 3, 16, 128)),
            shaped((2, 4, 3, 16, 128)),
            shaped((rank, 128), f32),
        ),
        in_specs=[pl.BlockSpec(memory_space=pltpu.SMEM)] + [far] * 10,
        out_specs=(close,) * 4,
        scratch_shapes=[
            VMEM((KVL + ROTARY_WIDTH, token_rows), bf), VMEM((4, token_rows // 4, 640), bf),
            VMEM((8, 128), jnp.int32), VMEM((4, token_rows // 4, 640), bf),
            VMEM((8, 128), jnp.int32), VMEM((128, 128), f32), VMEM((128, 128), f32),
            VMEM((SPAN, 4, token_rows // 4, 640), bf), VMEM((SPAN, 8, 128), jnp.int32),
            VMEM((4, 8, 2, held_columns, half_out), bf), VMEM((2, token_rows, width), bf),
            VMEM((2, token_rows, half_out), bf), VMEM((2, token_rows, half_out), bf),
            VMEM(frozen_queries.shape, bf), VMEM(query_latent_rows.shape, bf),
            VMEM((rank, query_latent_rows.shape[1]), bf), VMEM(query_adapter_second.shape, bf),
            VMEM((rank, held_rows), bf), VMEM((rank, width), bf), VMEM(latent_up_weight.shape, bf),
            VMEM((token_rows, plain), bf), VMEM((token_rows, turn), bf),
            VMEM((head_number, keys, 256), bf), VMEM((head_number, keys, 128), bf),
            VMEM((head_number, token_rows, keys), bf), VMEM((token_rows, held_rows), bf),
            VMEM(frozen_queries.shape, bf),
            VMEM((rank, 128), f32), VMEM((4, rank, 128), f32),
            VMEM((rank, 128), f32), VMEM((rank, 128), f32),
            VMEM((rank, 128), f32), VMEM((4, rank, 128), f32),
            VMEM((rank, 128), f32), VMEM((rank, 128), f32),
            *tree(8, 2, 4), *tree(3, 3, 3), *tree(3, 3, 3),
            DMA((5,)), DMA((7,)), DMA((7,)), DMA((7,)), DMA((7,)), DMA((3,)), DMA((3,)),
            DMA((3, 2)), DMA((3, 2)), DMA((2, 4, 4)), DMA((2, 4, 4)), DMA((2, 8)), DMA((2, 8)),
            DMA((8,)), DMA((8,)), DMA((8,)), DMA((8,)), DMA((3, 18)), DMA((3, 18)), DMA((10,)),
        ],
        compiler_params=pltpu.CompilerParams(
            collective_id=0, has_side_effects=True, vmem_limit_bytes=56 * 1024 * 1024
        ),
    )(
        block_starts, key_value_latent.T,
        frozen_output_weight.T, output_cotangent, frozen_queries, query_latent_rows,
        query_adapter_first.T, query_adapter_second, output_adapter_first.T,
        output_adapter_second, latent_up_weight,
    )
    grad_qa, grad_qb, grad_oa, grad_ob = pl.pallas_call(
        finish_kernel,
        out_shape=(
            shaped((rank, query_latent_rows.shape[1]), f32),
            shaped(query_adapter_second.shape, f32),
            shaped((rank, held_rows), f32),
            shaped((rank, held_columns), f32),
        ),
        in_specs=[close] * 4,
        out_specs=(close,) * 4,
    )(*pieces)
    return (grad_qa.T, grad_qb, grad_oa.T, grad_ob)


def solution(mesh):
    return jax.shard_map(
        body,
        mesh=mesh,
        in_specs=(
            P("ctx", "head"),
            P("ctx", None),
            P("ctx", None),
            P("ctx", None),
            P(None, "head"),
            P(),
            P(None, "head"),
            P("head", None),
            P(),
            P("head", "ctx"),
            P("ctx", None),
        ),
        out_specs=(P(), P(None, "head"), P("head", None), P(None, "ctx")),
        check_vma=False,
    )
```

```python
import math

import jax
import jax.numpy as jnp
from jax import lax
from jax.experimental import pallas as pl
from jax.experimental.pallas import tpu as pltpu
from jax.sharding import PartitionSpec as P

PLAIN_WIDTH = 128
ROTARY_WIDTH = 64
VALUE_WIDTH = 128
KVL = 512
SPAN = 8
ROPE_BASE = 10000.0
MESH = pl.DeviceIdType.MESH
VMEM = pltpu.VMEM
DMA = pltpu.SemaphoreType.DMA


def columns_contract(left, right):
    return lax.dot_general(
        left, right, (((1,), (1,)), ((), ())), preferred_element_type=jnp.float32
    )


def send(src, dst, send_sem, recv_sem, axis, target):
    copy = pltpu.make_async_remote_copy(
        src_ref=src,
        dst_ref=dst,
        send_sem=send_sem,
        recv_sem=recv_sem,
        device_id={axis: target},
        device_id_type=MESH,
    )
    copy.start()
    return copy


def places(place):
    core = lax.rem(place, 2)
    y = lax.rem(place // 2, 8)
    z = place // 16
    partner = place + 1 - 2 * core
    return core, y, z, partner


def dot(left, right):
    return jnp.dot(left, right, preferred_element_type=jnp.float32)


def turned(vectors, cosine, sine):
    lane = lax.broadcasted_iota(jnp.int32, vectors.shape, 1)
    other = jnp.where(
        lax.rem(lane, 64) < 32, pltpu.roll(vectors, 96, 1), pltpu.roll(vectors, 32, 1)
    )
    return vectors * cosine + other * sine


def tree_reduce(at, x, r1, t1, r2, t2, r3, g0, full, tail, send_sem, recv_sem, local_sem, sent):
    core, row, slot, partner, near, near_at, kin, kin_at, group_at = at
    kept = full.shape[2]

    def go(index, src, dst, target):
        copy = send(src, dst, send_sem.at[index], recv_sem.at[index], "ctx", target)
        sent.append(copy)
        return copy

    copy = go(0, x.at[1 - core], r1, partner)
    yield
    copy.wait_recv()
    t1[...] = (x[core].astype(jnp.float32) + r1[...].astype(jnp.float32)).astype(jnp.bfloat16)
    copies = [go(1 + i, t1.at[near[i]], r2.at[i], near_at[i]) for i in range(3)]
    yield
    total = x[core, row].astype(jnp.float32) + r1[row].astype(jnp.float32)
    for i, copy in enumerate(copies):
        copy.wait_recv()
        total = total + r2[i].astype(jnp.float32)
    total = total.astype(jnp.bfloat16)
    for i in range(8):
        t2[i, :kept] = total[:kept]
        if tail is not None:
            first = kept + 2 * (i // 3)
            t2[i, kept:] = total[first:first + 2]
    copies = [go(4 + i, t2.at[kin[i]], r3.at[slot], kin_at[i]) for i in range(7)]
    r3[slot] = t2[slot]
    yield
    for copy in copies:
        copy.wait_recv()
    total = r3[0].astype(jnp.float32)
    for i in range(1, 8):
        total = total + r3[i].astype(jnp.float32)
    if tail is not None:
        tail(total[kept:].reshape(32, 128))
    lead = total[:kept].astype(jnp.bfloat16)
    g0[...] = lead
    full[core, row] = lead
    copies = [go(11 + i, g0, full.at[core, row], group_at[i]) for i in range(7)]
    yield
    for copy in copies:
        copy.wait_recv()
    yield


def attend_kernel(
    starts_ref, kvt_ref,
    w_ref, cot_ref, fq_ref, ql_ref, qa_ref, qb_ref, oa_ref, ob_ref, up_ref,
    full_e, full_b, full_a, ob_out,
    kvt_s, kv_pre, place_pre, kv_ref, places_ref, cos_ref, sin_ref,
    kv_all, place_all, w_all, cot_all, d_mine, d_all,
    fq_s, ql_s, qa_s, qb_s, oa_s, ob_s, up_s,
    qn_s, qr_s, kcat_s, val_s, wt_s, att_s, grad_s,
    part_s, hx_s, hy_s, hz_s, po_s, ox_s, oy_s, oz_s,
    xe, re1, te1, re2, te2, re3, ge, xb, rb1, tb1, rb2, tb2, rb3, gb,
    xa, ra1, ta1, ra2, ta2, ra3, gq,
    local_sem, kv_s, kv_r, st_s, st_r, pair_s, pair_r, z_s, z_r, y_s, y_r, x_s, x_r, f_s, f_r,
    h_s, h_r, tree_s, tree_r, load_sem,
):
    place = lax.axis_index("ctx")
    core, y, z, partner = places(place)
    slot = place // 8
    head = lax.axis_index("head")
    x, block = lax.rem(head, 4), (head // 4) * 4
    right, left = block + lax.rem(x + 1, 4), block + lax.rem(x + 3, 4)
    kin = [lax.rem(place + 8 * step, 64) for step in range(1, SPAN)]
    up = z * 16 + lax.rem(y + 1, 8) * 2 + core
    down = z * 16 + lax.rem(y + 7, 8) * 2 + core
    row = lax.rem(y, 4)
    kin_slot = [lax.rem(slot + step, 8) for step in range(1, 8)]
    near = [lax.rem(row + step, 4) for step in range(1, 4)]
    near_at = [8 * slot + 2 * other + core for other in near]
    group_at = [8 * slot + lax.rem(lax.rem(place, 8) + step, 8) for step in range(1, 8)]
    beside = [block + lax.rem(x + step, 4) for step in range(1, 4)]
    facing = 4 - block + x
    barrier = pltpu.get_barrier_semaphore()
    for target in kin + group_at + [up, down]:
        pl.semaphore_signal(barrier, inc=1, device_id={"ctx": target}, device_id_type=MESH)
    for target in beside + [facing]:
        pl.semaphore_signal(barrier, inc=1, device_id={"head": target}, device_id_type=MESH)
    loads = [
        pltpu.make_async_copy(src, dst, load_sem.at[i])
        for i, (src, dst) in enumerate((
            (kvt_ref, kvt_s), (ql_ref, ql_s), (qa_ref, qa_s), (fq_ref, fq_s), (qb_ref, qb_s),
            (up_ref, up_s), (oa_ref, oa_s), (ob_ref, ob_s),
        ))
    ]
    for copy in loads:
        copy.start()
    start, middle = starts_ref[0, 0], starts_ref[0, 1]

    def spread(shape, axis):
        step = lax.broadcasted_iota(jnp.int32, shape, axis)
        return jnp.where(step < 64, step + start, step - 64 + middle)

    lane = lax.broadcasted_iota(jnp.int32, (128, 128), 1)
    power = lax.rem(lane, 32).astype(jnp.float32) * (-2.0 * math.log(ROPE_BASE) / ROTARY_WIDTH)
    angle = spread((128, 128), 0).astype(jnp.float32) * jnp.exp(power)
    cos_ref[...] = jnp.cos(angle)
    sine = jnp.sin(angle)
    sin_ref[...] = jnp.where(lax.rem(lane, 64) < 32, -sine, sine)
    place_pre[...] = spread((8, 128), 1)
    loads[0].wait()
    raw = kvt_s[KVL:].astype(jnp.float32)
    rope = turned(jnp.concatenate([raw, raw], 0).T, cos_ref[...], sin_ref[...])
    latent = kvt_s[:KVL].astype(jnp.float32).T
    kv_pre[:, :, :KVL] = latent.astype(jnp.bfloat16).reshape(4, 32, KVL)
    kv_pre[:, :, KVL:] = rope.astype(jnp.bfloat16).reshape(4, 32, 128)
    bounce = [
        pltpu.make_async_copy(kv_pre, kv_ref, load_sem.at[8]),
        pltpu.make_async_copy(place_pre, places_ref, load_sem.at[9]),
    ]
    for copy in bounce:
        copy.start()
    for copy in bounce:
        copy.wait()
    pl.semaphore_wait(barrier, len(kin) + len(group_at) + 6)
    mine = pl.ds(pl.multiple_of(core * 512, 512), 512)
    theirs = pl.ds(pl.multiple_of((1 - core) * 512, 512), 512)

    own = [
        pltpu.make_async_copy(kv_ref.at[x], kv_all.at[slot, x], local_sem.at[0]),
        pltpu.make_async_copy(places_ref, place_all.at[slot], local_sem.at[1]),
        pltpu.make_async_copy(w_ref.at[:, mine], w_all.at[z, y, core], local_sem.at[2]),
        pltpu.make_async_copy(cot_ref, cot_all.at[core], local_sem.at[3]),
    ]
    for copy in own:
        copy.start()
    pending = []
    swap_w = send(
        w_ref.at[:, theirs], w_all.at[z, y, core], pair_s.at[0], pair_r.at[0], "ctx", partner
    )
    first = []
    for step in range(1, SPAN):
        i = step - 1
        first.append(send(kv_ref.at[x], kv_all.at[slot, x], kv_s.at[i], kv_r.at[i], "ctx", kin[i]))
    for i in range(SPAN - 1):
        pending.append(
            send(places_ref, place_all.at[slot], st_s.at[i], st_r.at[i], "ctx", kin[i])
        )
    swap_cot = send(cot_ref, cot_all.at[core], pair_s.at[1], pair_r.at[1], "ctx", partner)
    pending.append(swap_cot)
    across = [
        [
            send(kv_ref.at[x], kv_all.at[slot, x], x_s.at[side, 0], x_r.at[side, 0], "head", target)
        ]
        for side, target in ((0, right), (1, left))
    ]
    line = []
    for step in range(1, 4):
        target = lax.rem(z + step, 4) * 16 + y * 2 + core
        line.append([
            send(
                w_ref.at[:, mine], w_all.at[z, y, core],
                z_s.at[step - 1, 0], z_r.at[step - 1, 0], "ctx", target,
            )
        ])

    for copy in loads[1:5]:
        copy.wait()
    low = columns_contract(ql_s[...], qa_s[...]).astype(jnp.bfloat16)
    low_turned = columns_contract(qa_s[...], ql_s[...]).astype(jnp.bfloat16)
    early = lax.broadcasted_iota(jnp.int32, (low.shape[0], 128), 1) < 64
    for pair in range(4):
        lanes = slice(384 * pair, 384 * pair + 384)
        vectors = fq_s[:, lanes].astype(jnp.float32) + dot(low, qb_s[:, lanes])
        one, two, three = [vectors[:, 128 * i:128 * i + 128] for i in range(3)]
        qn_s[:, 256 * pair:256 * pair + 128] = one.astype(jnp.bfloat16)
        qn_s[:, 256 * pair + 128:256 * pair + 256] = jnp.where(
            early, pltpu.roll(two, 64, 1), pltpu.roll(three, 64, 1)
        ).astype(jnp.bfloat16)
        qr_s[:, 128 * pair:128 * pair + 128] = turned(
            jnp.where(early, two, three), cos_ref[...], sin_ref[...]
        ).astype(jnp.bfloat16)

    swap_w.wait_recv()
    for step in range(1, 4):
        target = lax.rem(z + step, 4) * 16 + y * 2 + core
        line[step - 1].append(
            send(
                w_all.at[z, y, 1 - core], w_all.at[z, y, 1 - core],
                z_s.at[step - 1, 1], z_r.at[step - 1, 1], "ctx", target,
            )
        )
    own[2].wait()
    rings = {}

    def ring(step, unit):
        depth = lax.rem(z - unit + 4, 4)
        if step == 1 and unit:
            line[unit - 1][0].wait_recv()
            line[unit - 1][1].wait_recv()
        for side, target in ((0, up), (1, down)):
            if step > 1 and (side, step - 1, unit) in rings:
                rings[side, step - 1, unit].wait_recv()
            if step == 5 or (step == 4 and (unit // 2) != side):
                continue
            shift = -(step - 1) if side == 0 else step - 1
            column = lax.rem(y + shift + 8, 8)
            rings[side, step, unit] = send(
                w_all.at[depth, column], w_all.at[depth, column],
                y_s.at[side, step - 1, unit], y_r.at[side, step - 1, unit], "ctx", target,
            )

    ring(1, 0)
    for i in range(SPAN - 1):
        first[i].wait_recv()
        source = lax.rem(slot + 7 - i, 8)
        for side, target in ((0, right), (1, left)):
            across[side].append(
                send(
                    kv_all.at[source, x], kv_all.at[source, x],
                    x_s.at[side, i + 1], x_r.at[side, i + 1], "head", target,
                )
            )
    for unit in range(1, 4):
        ring(1, unit)
    relays = []
    for i in range(SPAN):
        source = lax.rem(slot + 8 - i, 8)
        across[0][i].wait_recv()
        across[1][i].wait_recv()
        if i % 2 == 0:
            target, lane = right, lax.rem(x + 3, 4)
        else:
            target, lane = left, lax.rem(x + 1, 4)
        relays.append(
            send(
                kv_all.at[source, lane], kv_all.at[source, lane],
                f_s.at[i], f_r.at[i], "head", target,
            )
        )
        if i % 2:
            ring(2, i // 2)
    own[0].wait()
    own[1].wait()
    for copy in relays + pending[:SPAN - 1]:
        copy.wait_recv()

    for copy in loads[5:]:
        copy.wait()
    positions = jnp.concatenate([place_all[i, 0:1, :] for i in range(SPAN)], 1)
    keys = positions.shape[1]
    visible = positions <= spread((128, 1), 0)
    latents = kv_all[...].reshape(keys, 640)
    rope2 = latents[:, KVL:]
    scale = (PLAIN_WIDTH + ROTARY_WIDTH) ** (-0.5)
    lane_half = lax.broadcasted_iota(jnp.int32, (qr_s.shape[0], 128), 1) // 64

    def forward(number, total):
        kv = dot(latents[:, :KVL], up_s[:, pl.ds(pl.multiple_of(number * 256, 256), 256)])
        kv = kv.astype(jnp.bfloat16)
        kcat_s[number, :, :128] = kv[:, :128]
        kcat_s[number, :, 128:] = rope2
        val_s[number] = kv[:, 128:]
        plain = qn_s[:, pl.ds(pl.multiple_of(number * 128, 128), 128)]
        turn = qr_s[:, pl.ds(pl.multiple_of((number // 2) * 128, 128), 128)].astype(jnp.float32)
        turn = jnp.where(lane_half == lax.rem(number, 2), turn, 0.0).astype(jnp.bfloat16)
        query = jnp.concatenate([plain, turn], 1)
        scores = columns_contract(query, kcat_s[number]) * scale
        scores = jnp.where(visible, scores, -jnp.inf)
        expo = jnp.exp(scores - jnp.max(scores, -1, keepdims=True))
        weights = (expo * (1.0 / jnp.sum(expo, -1, keepdims=True))).astype(jnp.bfloat16)
        wt_s[number] = weights
        attended = dot(weights, val_s[number]).astype(jnp.bfloat16)
        att_s[:, pl.ds(pl.multiple_of(number * 128, 128), 128)] = attended
        return total + columns_contract(
            oa_s[:, pl.ds(pl.multiple_of(number * 128, 128), 128)], attended
        )

    total = jnp.zeros((32, 128), jnp.float32)
    served = [
        [(3, 0), (3, 1), (3, 2)], [(3, 3)], [(4, 0)], [(4, 1), (4, 2)], [(4, 3)], [], [],
        [(5, 0), (5, 1), (5, 2), (5, 3)],
    ]
    done = 0
    for number, turns in enumerate(served):
        if turns:
            total = lax.fori_loop(done, number + 1, forward, total)
            done = number + 1
        for step, unit in turns:
            ring(step, unit)
    po_s[...] = total
    ox_s[x] = total
    heads = [send(po_s, ox_s.at[x], h_s.at[i], h_r.at[i], "head", beside[i]) for i in range(3)]
    swap_cot.wait_recv()
    own[3].wait()

    tokens, half_out = d_mine.shape[1], d_mine.shape[2]
    cot = cot_all[...].reshape(2 * tokens, cot_all.shape[2])
    rank = columns_contract(cot, ob_s[...]).astype(jnp.bfloat16)
    d_half = dot(cot, w_all[...].reshape(cot.shape[1], half_out)) + dot(rank, oa_s[:, mine])
    d_mine[...] = d_half.astype(jnp.bfloat16).reshape(d_mine.shape)
    swap_d = send(
        d_mine.at[1 - core], d_all.at[core], pair_s.at[2], pair_r.at[2], "ctx", partner
    )
    keep = pltpu.make_async_copy(d_mine.at[core], d_all.at[core], local_sem.at[4])
    keep.start()
    rank_turned = columns_contract(ob_s[...], cot_all[core]).astype(jnp.bfloat16)
    oa_term = dot(rank_turned, att_s[...]).astype(jnp.bfloat16)
    for unit in range(16):
        high, tile = unit // 8, unit % 8
        xe[unit // 8, unit // 2 % 4, unit % 2] = oa_term[
            16 * high:16 * high + 16, 128 * tile:128 * tile + 128
        ]
    for copy in heads:
        copy.wait_recv()
    oy_s[...] = ox_s[0] + ox_s[1] + ox_s[2] + ox_s[3]
    heads.append(send(oy_s, oz_s, h_s.at[3], h_r.at[3], "head", facing))
    swap_d.wait_recv()
    keep.wait()
    at = (core, row, slot, partner, near, near_at, kin_slot, kin, group_at)
    sent = []

    def backward(pair, total):
        turns, plains = [], []
        for even in range(2):
            number = 2 * pair + even
            lanes = pl.ds(pl.multiple_of(lax.rem(number, 4) * 128, 128), 128)
            d_prob = columns_contract(d_all[number // 4, :, lanes], val_s[number])
            weights = wt_s[number].astype(jnp.float32)
            delta = jnp.sum(weights * d_prob, -1, keepdims=True)
            d_score = (weights * (d_prob - delta) * scale).astype(jnp.bfloat16)
            grad = dot(d_score, kcat_s[number])
            plains.append(grad[:, :128])
            turns.append(turned(grad[:, 128:], cos_ref[...], -sin_ref[...]))
        turn = jnp.where(early, turns[0], turns[1])
        moved = pltpu.roll(plains[1], 64, 1)
        parts = [plains[0], jnp.where(early, turn, moved), jnp.where(early, moved, turn)]
        for i, piece in enumerate(parts):
            at = pl.ds(pl.multiple_of(pair * 384 + i * 128, 128), 128)
            piece = piece.astype(jnp.bfloat16)
            grad_s[:, at] = piece
            total = total + columns_contract(qb_s[:, at], piece)
        return total

    total = lax.fori_loop(0, 2, backward, jnp.zeros((32, 128), jnp.float32))
    heads[3].wait_recv()
    o_low = (oy_s[...] + oz_s[...]).astype(jnp.bfloat16)
    ob_term = dot(o_low, cot_all[core])
    lane = lax.broadcasted_iota(jnp.int32, (32, 128), 1)

    def shifted(start, to):
        tile, offset = start // 128, start % 128
        shift = (to - offset) % 128
        value = pltpu.roll(ob_term[:, 128 * tile:128 * tile + 128], shift, 1)
        if offset + 40 > 128:
            after = pltpu.roll(ob_term[:, 128 * tile + 128:128 * tile + 256], shift, 1)
            value = jnp.where(lane < to + 128 - offset, value, after)
        return value

    for half in range(2):
        for line_row in range(4):
            for third in range(3):
                packed = jnp.zeros((32, 128), jnp.float32)
                for i in range(3):
                    member = 3 * third + i
                    if member > 7:
                        continue
                    value = shifted(40 * (8 * member + 2 * line_row + half), 40 * i)
                    inside = (lane >= 40 * i) & (lane < 40 * i + 40)
                    packed = jnp.where(inside, value, packed)
                packed = packed.astype(jnp.bfloat16)
                xe[half, line_row, 2 + 2 * third] = packed[:16]
                xe[half, line_row, 3 + 2 * third] = packed[16:]

    def tail(total):
        third = lax.rem(slot, 3)
        value = jnp.where(third == 1, pltpu.roll(total, 88, 1), total)
        value = jnp.where(third == 2, pltpu.roll(total, 48, 1), value)
        ob_out[...] = value

    soon = tree_reduce(
        at, xe, re1, te1, re2, te2, re3, ge, full_e, tail,
        tree_s.at[0], tree_r.at[0], None, sent,
    )
    next(soon)
    total = lax.fori_loop(2, 3, backward, total)
    next(soon)
    total = lax.fori_loop(3, 4, backward, total)
    part_s[...] = total
    hx_s[x] = total
    late = [
        send(part_s, hx_s.at[x], h_s.at[4 + i], h_r.at[4 + i], "head", beside[i]) for i in range(3)
    ]
    next(soon)
    qb_term = dot(low_turned, grad_s[...]).astype(jnp.bfloat16)
    for unit in range(24):
        high, tile = unit // 12, unit % 12
        xb[unit // 12, unit // 3 % 4, unit % 3] = qb_term[
            16 * high:16 * high + 16, 128 * tile:128 * tile + 128
        ]
    wide = tree_reduce(
        at, xb, rb1, tb1, rb2, tb2, rb3, gb, full_b, None,
        tree_s.at[1], tree_r.at[1], None, sent,
    )
    next(wide)
    for copy in late:
        copy.wait_recv()
    hy_s[...] = hx_s[0] + hx_s[1] + hx_s[2] + hx_s[3]
    late.append(send(hy_s, hz_s, h_s.at[7], h_r.at[7], "head", facing))
    next(wide)
    next(soon)
    late[3].wait_recv()
    sums = (hy_s[...] + hz_s[...]).astype(jnp.bfloat16)
    qa_term = dot(sums, ql_s[...]).astype(jnp.bfloat16)
    for unit in range(24):
        high, tile = unit // 12, unit % 12
        xa[unit // 12, unit // 3 % 4, unit % 3] = qa_term[
            16 * high:16 * high + 16, 128 * tile:128 * tile + 128
        ]
    slim = tree_reduce(
        at, xa, ra1, ta1, ra2, ta2, ra3, gq, full_a, None,
        tree_s.at[2], tree_r.at[2], None, sent,
    )
    next(slim)
    next(slim)
    next(wide)
    next(slim)
    next(wide)
    next(soon)
    next(slim)
    next(wide)
    next(slim)
    heads += late

    done = first + pending + [swap_w, swap_d] + line[0] + line[1] + line[2] + heads + sent
    for copy in done + across[0] + across[1] + relays + list(rings.values()):
        copy.wait_send()


def finish_kernel(full_e, full_b, full_a, tail_ref, qa_out, qb_out, oa_out, ob_out):
    for source, out, kept in ((full_a, qa_out, 3), (full_b, qb_out, 3), (full_e, oa_out, 2)):
        tiles = out.shape[1] // 128
        for unit in range(8 * kept):
            high, tile = unit // tiles, unit % tiles
            out[16 * high:16 * high + 16, 128 * tile:128 * tile + 128] = source[
                unit // (4 * kept), unit // kept % 4, unit % kept
            ].astype(jnp.float32)
    ob_out[...] = tail_ref[...][:, :40]


def shaped(shape, dtype=jnp.bfloat16):
    return jax.ShapeDtypeStruct(shape, dtype)


def body(
    frozen_queries,
    query_latent_rows,
    key_value_latent,
    block_starts,
    latent_up_weight,
    query_adapter_first,
    query_adapter_second,
    output_adapter_first,
    output_adapter_second,
    frozen_output_weight,
    output_cotangent,
):
    token_rows = frozen_queries.shape[0]
    per_head_width = PLAIN_WIDTH + ROTARY_WIDTH
    head_number = query_adapter_second.shape[1] // per_head_width
    width = output_cotangent.shape[1]
    rank = query_adapter_first.shape[1]
    held_rows, held_columns = frozen_output_weight.shape
    half_out = held_rows // 2
    bf = jnp.bfloat16
    keys = SPAN * token_rows
    plain, turn = head_number * PLAIN_WIDTH, head_number * ROTARY_WIDTH

    def tree(used, kept, deep):
        return [
            VMEM((2, 4, used, 16, 128), bf), VMEM((4, used, 16, 128), bf),
            VMEM((4, used, 16, 128), bf), VMEM((3, used, 16, 128), bf),
            VMEM((8, deep, 16, 128), bf), VMEM((8, deep, 16, 128), bf), VMEM((kept, 16, 128), bf),
        ]

    close, far = pl.BlockSpec(memory_space=VMEM), pl.BlockSpec(memory_space=pltpu.HBM)
    f32 = jnp.float32
    pieces = pl.pallas_call(
        attend_kernel,
        out_shape=(
            shaped((2, 4, 2, 16, 128)),
            shaped((2, 4, 3, 16, 128)),
            shaped((2, 4, 3, 16, 128)),
            shaped((rank, 128), f32),
        ),
        in_specs=[pl.BlockSpec(memory_space=pltpu.SMEM)] + [far] * 10,
        out_specs=(close,) * 4,
        scratch_shapes=[
            VMEM((KVL + ROTARY_WIDTH, token_rows), bf), VMEM((4, token_rows // 4, 640), bf),
            VMEM((8, 128), jnp.int32), VMEM((4, token_rows // 4, 640), bf),
            VMEM((8, 128), jnp.int32), VMEM((128, 128), f32), VMEM((128, 128), f32),
            VMEM((SPAN, 4, token_rows // 4, 640), bf), VMEM((SPAN, 8, 128), jnp.int32),
            VMEM((4, 8, 2, held_columns, half_out), bf), VMEM((2, token_rows, width), bf),
            VMEM((2, token_rows, half_out), bf), VMEM((2, token_rows, half_out), bf),
            VMEM(frozen_queries.shape, bf), VMEM(query_latent_rows.shape, bf),
            VMEM((rank, query_latent_rows.shape[1]), bf), VMEM(query_adapter_second.shape, bf),
            VMEM((rank, held_rows), bf), VMEM((rank, width), bf), VMEM(latent_up_weight.shape, bf),
            VMEM((token_rows, plain), bf), VMEM((token_rows, turn), bf),
            VMEM((head_number, keys, 256), bf), VMEM((head_number, keys, 128), bf),
            VMEM((head_number, token_rows, keys), bf), VMEM((token_rows, held_rows), bf),
            VMEM(frozen_queries.shape, bf),
            VMEM((rank, 128), f32), VMEM((4, rank, 128), f32),
            VMEM((rank, 128), f32), VMEM((rank, 128), f32),
            VMEM((rank, 128), f32), VMEM((4, rank, 128), f32),
            VMEM((rank, 128), f32), VMEM((rank, 128), f32),
            *tree(8, 2, 4), *tree(3, 3, 3), *tree(3, 3, 3),
            DMA((5,)), DMA((7,)), DMA((7,)), DMA((7,)), DMA((7,)), DMA((3,)), DMA((3,)),
            DMA((3, 2)), DMA((3, 2)), DMA((2, 4, 4)), DMA((2, 4, 4)), DMA((2, 8)), DMA((2, 8)),
            DMA((8,)), DMA((8,)), DMA((8,)), DMA((8,)), DMA((3, 18)), DMA((3, 18)), DMA((10,)),
        ],
        compiler_params=pltpu.CompilerParams(
            collective_id=0, has_side_effects=True, vmem_limit_bytes=56 * 1024 * 1024
        ),
    )(
        block_starts, key_value_latent.T,
        frozen_output_weight.T, output_cotangent, frozen_queries, query_latent_rows,
        query_adapter_first.T, query_adapter_second, output_adapter_first.T,
        output_adapter_second, latent_up_weight,
    )
    grad_qa, grad_qb, grad_oa, grad_ob = pl.pallas_call(
        finish_kernel,
        out_shape=(
            shaped((rank, query_latent_rows.shape[1]), f32),
            shaped(query_adapter_second.shape, f32),
            shaped((rank, held_rows), f32),
            shaped((rank, held_columns), f32),
        ),
        in_specs=[close] * 4,
        out_specs=(close,) * 4,
    )(*pieces)
    return (grad_qa.T, grad_qb, grad_oa.T, grad_ob)


def solution(mesh):
    return jax.shard_map(
        body,
        mesh=mesh,
        in_specs=(
            P("ctx", "head"),
            P("ctx", None),
            P("ctx", None),
            P("ctx", None),
            P(None, "head"),
            P(),
            P(None, "head"),
            P("head", None),
            P(),
            P("head", "ctx"),
            P("ctx", None),
        ),
        out_specs=(P(), P(None, "head"), P("head", None), P(None, "ctx")),
        check_vma=False,
    )
```

```python
import math

import jax
import jax.numpy as jnp
from jax import lax
from jax.experimental import pallas as pl
from jax.experimental.pallas import tpu as pltpu
from jax.sharding import PartitionSpec as P

PLAIN_WIDTH = 128
ROTARY_WIDTH = 64
VALUE_WIDTH = 128
KVL = 512
SPAN = 8
ROPE_BASE = 10000.0
MESH = pl.DeviceIdType.MESH
VMEM = pltpu.VMEM
DMA = pltpu.SemaphoreType.DMA


def columns_contract(left, right):
    return lax.dot_general(
        left, right, (((1,), (1,)), ((), ())), preferred_element_type=jnp.float32
    )


def send(src, dst, send_sem, recv_sem, axis, target):
    copy = pltpu.make_async_remote_copy(
        src_ref=src,
        dst_ref=dst,
        send_sem=send_sem,
        recv_sem=recv_sem,
        device_id={axis: target},
        device_id_type=MESH,
    )
    copy.start()
    return copy


def places(place):
    core = lax.rem(place, 2)
    y = lax.rem(place // 2, 8)
    z = place // 16
    partner = place + 1 - 2 * core
    return core, y, z, partner


def dot(left, right):
    return jnp.dot(left, right, preferred_element_type=jnp.float32)


def turned(vectors, cosine, sine):
    lane = lax.broadcasted_iota(jnp.int32, vectors.shape, 1)
    other = jnp.where(
        lax.rem(lane, 64) < 32, pltpu.roll(vectors, 96, 1), pltpu.roll(vectors, 32, 1)
    )
    return vectors * cosine + other * sine


def tree_reduce(at, x, r1, t1, r2, t2, r3, g0, full, tail, send_sem, recv_sem, local_sem, sent):
    core, row, slot, partner, near, near_at, kin, kin_at, group_at = at
    kept = full.shape[2]

    def go(index, src, dst, target):
        copy = send(src, dst, send_sem.at[index], recv_sem.at[index], "ctx", target)
        sent.append(copy)
        return copy

    copy = go(0, x.at[1 - core], r1, partner)
    yield
    copy.wait_recv()
    t1[...] = (x[core].astype(jnp.float32) + r1[...].astype(jnp.float32)).astype(jnp.bfloat16)
    copies = [go(1 + i, t1.at[near[i]], r2.at[i], near_at[i]) for i in range(3)]
    yield
    total = x[core, row].astype(jnp.float32) + r1[row].astype(jnp.float32)
    for i, copy in enumerate(copies):
        copy.wait_recv()
        total = total + r2[i].astype(jnp.float32)
    total = total.astype(jnp.bfloat16)
    for i in range(8):
        t2[i, :kept] = total[:kept]
        if tail is not None:
            first = kept + 2 * (i // 3)
            t2[i, kept:] = total[first:first + 2]
    copies = [go(4 + i, t2.at[kin[i]], r3.at[slot], kin_at[i]) for i in range(7)]
    r3[slot] = t2[slot]
    yield
    for copy in copies:
        copy.wait_recv()
    total = r3[0].astype(jnp.float32)
    for i in range(1, 8):
        total = total + r3[i].astype(jnp.float32)
    if tail is not None:
        tail(total[kept:].reshape(32, 128))
    lead = total[:kept].astype(jnp.bfloat16)
    g0[...] = lead
    full[core, row] = lead
    copies = [go(11 + i, g0, full.at[core, row], group_at[i]) for i in range(7)]
    yield
    for copy in copies:
        copy.wait_recv()
    yield


def attend_kernel(
    starts_ref, kvt_ref,
    w_ref, cot_ref, fq_ref, ql_ref, qa_ref, qb_ref, oa_ref, ob_ref, up_ref,
    full_e, full_b, full_a, ob_out,
    kvt_s, kv_pre, place_pre, kv_ref, places_ref, cos_ref, sin_ref,
    kv_all, place_all, w_all, cot_all, d_mine, d_all,
    fq_s, ql_s, qa_s, qb_s, oa_s, ob_s, up_s,
    qn_s, qr_s, kcat_s, val_s, wt_s, att_s, grad_s,
    part_s, hx_s, hy_s, hz_s, po_s, ox_s, oy_s, oz_s,
    xe, re1, te1, re2, te2, re3, ge, xb, rb1, tb1, rb2, tb2, rb3, gb,
    xa, ra1, ta1, ra2, ta2, ra3, gq,
    local_sem, kv_s, kv_r, st_s, st_r, pair_s, pair_r, z_s, z_r, y_s, y_r, x_s, x_r, f_s, f_r,
    h_s, h_r, tree_s, tree_r, load_sem,
):
    place = lax.axis_index("ctx")
    core, y, z, partner = places(place)
    slot = place // 8
    head = lax.axis_index("head")
    x, block = lax.rem(head, 4), (head // 4) * 4
    right, left = block + lax.rem(x + 1, 4), block + lax.rem(x + 3, 4)
    kin = [lax.rem(place + 8 * step, 64) for step in range(1, SPAN)]
    up = z * 16 + lax.rem(y + 1, 8) * 2 + core
    down = z * 16 + lax.rem(y + 7, 8) * 2 + core
    row = lax.rem(y, 4)
    kin_slot = [lax.rem(slot + step, 8) for step in range(1, 8)]
    near = [lax.rem(row + step, 4) for step in range(1, 4)]
    near_at = [8 * slot + 2 * other + core for other in near]
    group_at = [8 * slot + lax.rem(lax.rem(place, 8) + step, 8) for step in range(1, 8)]
    beside = [block + lax.rem(x + step, 4) for step in range(1, 4)]
    facing = 4 - block + x
    barrier = pltpu.get_barrier_semaphore()
    for target in kin + group_at + [up, down]:
        pl.semaphore_signal(barrier, inc=1, device_id={"ctx": target}, device_id_type=MESH)
    for target in beside + [facing]:
        pl.semaphore_signal(barrier, inc=1, device_id={"head": target}, device_id_type=MESH)
    loads = [
        pltpu.make_async_copy(src, dst, load_sem.at[i])
        for i, (src, dst) in enumerate((
            (kvt_ref, kvt_s), (ql_ref, ql_s), (qa_ref, qa_s), (fq_ref, fq_s), (qb_ref, qb_s),
            (up_ref, up_s), (oa_ref, oa_s), (ob_ref, ob_s),
        ))
    ]
    for copy in loads:
        copy.start()
    start, middle = starts_ref[0, 0], starts_ref[0, 1]

    def spread(shape, axis):
        step = lax.broadcasted_iota(jnp.int32, shape, axis)
        return jnp.where(step < 64, step + start, step - 64 + middle)

    lane = lax.broadcasted_iota(jnp.int32, (128, 128), 1)
    power = lax.rem(lane, 32).astype(jnp.float32) * (-2.0 * math.log(ROPE_BASE) / ROTARY_WIDTH)
    angle = spread((128, 128), 0).astype(jnp.float32) * jnp.exp(power)
    cos_ref[...] = jnp.cos(angle)
    sine = jnp.sin(angle)
    sin_ref[...] = jnp.where(lax.rem(lane, 64) < 32, -sine, sine)
    place_pre[...] = spread((8, 128), 1)
    loads[0].wait()
    raw = kvt_s[KVL:].astype(jnp.float32)
    rope = turned(jnp.concatenate([raw, raw], 0).T, cos_ref[...], sin_ref[...])
    latent = kvt_s[:KVL].astype(jnp.float32).T
    kv_pre[:, :, :KVL] = latent.astype(jnp.bfloat16).reshape(4, 32, KVL)
    kv_pre[:, :, KVL:] = rope.astype(jnp.bfloat16).reshape(4, 32, 128)
    bounce = [
        pltpu.make_async_copy(kv_pre, kv_ref, load_sem.at[8]),
        pltpu.make_async_copy(place_pre, places_ref, load_sem.at[9]),
    ]
    for copy in bounce:
        copy.start()
    for copy in bounce:
        copy.wait()
    pl.semaphore_wait(barrier, len(kin) + len(group_at) + 6)
    mine = pl.ds(pl.multiple_of(core * 512, 512), 512)
    theirs = pl.ds(pl.multiple_of((1 - core) * 512, 512), 512)

    own = [
        pltpu.make_async_copy(kv_ref.at[x], kv_all.at[slot, x], local_sem.at[0]),
        pltpu.make_async_copy(places_ref, place_all.at[slot], local_sem.at[1]),
        pltpu.make_async_copy(w_ref.at[:, mine], w_all.at[z, y, core], local_sem.at[2]),
        pltpu.make_async_copy(cot_ref, cot_all.at[core], local_sem.at[3]),
    ]
    for copy in own:
        copy.start()
    pending = []
    swap_w = send(
        w_ref.at[:, theirs], w_all.at[z, y, core], pair_s.at[0], pair_r.at[0], "ctx", partner
    )
    first = []
    for step in range(1, SPAN):
        i = step - 1
        first.append(send(kv_ref.at[x], kv_all.at[slot, x], kv_s.at[i], kv_r.at[i], "ctx", kin[i]))
    for i in range(SPAN - 1):
        pending.append(
            send(places_ref, place_all.at[slot], st_s.at[i], st_r.at[i], "ctx", kin[i])
        )
    swap_cot = send(cot_ref, cot_all.at[core], pair_s.at[1], pair_r.at[1], "ctx", partner)
    pending.append(swap_cot)
    across = [
        [
            send(kv_ref.at[x], kv_all.at[slot, x], x_s.at[side, 0], x_r.at[side, 0], "head", target)
        ]
        for side, target in ((0, right), (1, left))
    ]
    line = []
    for step in range(1, 4):
        target = lax.rem(z + step, 4) * 16 + y * 2 + core
        line.append([
            send(
                w_ref.at[:, mine], w_all.at[z, y, core],
                z_s.at[step - 1, 0], z_r.at[step - 1, 0], "ctx", target,
            )
        ])

    for copy in loads[1:5]:
        copy.wait()
    low = columns_contract(ql_s[...], qa_s[...]).astype(jnp.bfloat16)
    low_turned = columns_contract(qa_s[...], ql_s[...]).astype(jnp.bfloat16)
    early = lax.broadcasted_iota(jnp.int32, (low.shape[0], 128), 1) < 64
    for pair in range(4):
        lanes = slice(384 * pair, 384 * pair + 384)
        vectors = fq_s[:, lanes].astype(jnp.float32) + dot(low, qb_s[:, lanes])
        one, two, three = [vectors[:, 128 * i:128 * i + 128] for i in range(3)]
        qn_s[:, 256 * pair:256 * pair + 128] = one.astype(jnp.bfloat16)
        qn_s[:, 256 * pair + 128:256 * pair + 256] = jnp.where(
            early, pltpu.roll(two, 64, 1), pltpu.roll(three, 64, 1)
        ).astype(jnp.bfloat16)
        qr_s[:, 128 * pair:128 * pair + 128] = turned(
            jnp.where(early, two, three), cos_ref[...], sin_ref[...]
        ).astype(jnp.bfloat16)

    swap_w.wait_recv()
    for step in range(1, 4):
        target = lax.rem(z + step, 4) * 16 + y * 2 + core
        line[step - 1].append(
            send(
                w_all.at[z, y, 1 - core], w_all.at[z, y, 1 - core],
                z_s.at[step - 1, 1], z_r.at[step - 1, 1], "ctx", target,
            )
        )
    own[2].wait()
    rings = {}

    def ring(step, unit):
        depth = lax.rem(z - unit + 4, 4)
        if step == 1 and unit:
            line[unit - 1][0].wait_recv()
            line[unit - 1][1].wait_recv()
        for side, target in ((0, up), (1, down)):
            if step > 1 and (side, step - 1, unit) in rings:
                rings[side, step - 1, unit].wait_recv()
            if step == 5 or (step == 4 and (unit // 2) != side):
                continue
            shift = -(step - 1) if side == 0 else step - 1
            column = lax.rem(y + shift + 8, 8)
            rings[side, step, unit] = send(
                w_all.at[depth, column], w_all.at[depth, column],
                y_s.at[side, step - 1, unit], y_r.at[side, step - 1, unit], "ctx", target,
            )

    ring(1, 0)
    for i in (1, 3, 5, 0, 2, 4, 6):
        first[i].wait_recv()
        source = lax.rem(slot + 7 - i, 8)
        for side, target in ((0, right), (1, left)):
            across[side].append(
                send(
                    kv_all.at[source, x], kv_all.at[source, x],
                    x_s.at[side, i + 1], x_r.at[side, i + 1], "head", target,
                )
            )
    for unit in range(1, 4):
        ring(1, unit)
    relays = []
    for turn, i in enumerate((0, 2, 4, 6, 1, 3, 5, 7)):
        source = lax.rem(slot + 8 - i, 8)
        across[0][turn].wait_recv()
        across[1][turn].wait_recv()
        if turn % 2 == 0:
            target, lane = right, lax.rem(x + 3, 4)
        else:
            target, lane = left, lax.rem(x + 1, 4)
        relays.append(
            send(
                kv_all.at[source, lane], kv_all.at[source, lane],
                f_s.at[i], f_r.at[i], "head", target,
            )
        )
        if turn % 2:
            ring(2, turn // 2)
    own[0].wait()
    own[1].wait()
    for copy in relays + pending[:SPAN - 1]:
        copy.wait_recv()

    for copy in loads[5:]:
        copy.wait()
    positions = jnp.concatenate([place_all[i, 0:1, :] for i in range(SPAN)], 1)
    keys = positions.shape[1]
    visible = positions <= spread((128, 1), 0)
    latents = kv_all[...].reshape(keys, 640)
    rope2 = latents[:, KVL:]
    scale = (PLAIN_WIDTH + ROTARY_WIDTH) ** (-0.5)
    lane_half = lax.broadcasted_iota(jnp.int32, (qr_s.shape[0], 128), 1) // 64

    def forward(number, total):
        kv = dot(latents[:, :KVL], up_s[:, pl.ds(pl.multiple_of(number * 256, 256), 256)])
        kv = kv.astype(jnp.bfloat16)
        kcat_s[number, :, :128] = kv[:, :128]
        kcat_s[number, :, 128:] = rope2
        val_s[number] = kv[:, 128:]
        plain = qn_s[:, pl.ds(pl.multiple_of(number * 128, 128), 128)]
        turn = qr_s[:, pl.ds(pl.multiple_of((number // 2) * 128, 128), 128)].astype(jnp.float32)
        turn = jnp.where(lane_half == lax.rem(number, 2), turn, 0.0).astype(jnp.bfloat16)
        query = jnp.concatenate([plain, turn], 1)
        scores = columns_contract(query, kcat_s[number]) * scale
        scores = jnp.where(visible, scores, -jnp.inf)
        expo = jnp.exp(scores - jnp.max(scores, -1, keepdims=True))
        weights = (expo * (1.0 / jnp.sum(expo, -1, keepdims=True))).astype(jnp.bfloat16)
        wt_s[number] = weights
        attended = dot(weights, val_s[number]).astype(jnp.bfloat16)
        att_s[:, pl.ds(pl.multiple_of(number * 128, 128), 128)] = attended
        return total + columns_contract(
            oa_s[:, pl.ds(pl.multiple_of(number * 128, 128), 128)], attended
        )

    total = jnp.zeros((32, 128), jnp.float32)
    served = [
        [(3, 0), (3, 1), (3, 2)], [(3, 3)], [(4, 0)], [(4, 1), (4, 2)], [(4, 3)], [], [],
        [(5, 0), (5, 1), (5, 2), (5, 3)],
    ]
    done = 0
    for number, turns in enumerate(served):
        if turns:
            total = lax.fori_loop(done, number + 1, forward, total)
            done = number + 1
        for step, unit in turns:
            ring(step, unit)
    po_s[...] = total
    ox_s[x] = total
    heads = [send(po_s, ox_s.at[x], h_s.at[i], h_r.at[i], "head", beside[i]) for i in range(3)]
    swap_cot.wait_recv()
    own[3].wait()

    tokens, half_out = d_mine.shape[1], d_mine.shape[2]
    cot = cot_all[...].reshape(2 * tokens, cot_all.shape[2])
    rank = columns_contract(cot, ob_s[...]).astype(jnp.bfloat16)
    d_half = dot(cot, w_all[...].reshape(cot.shape[1], half_out)) + dot(rank, oa_s[:, mine])
    d_mine[...] = d_half.astype(jnp.bfloat16).reshape(d_mine.shape)
    swap_d = send(
        d_mine.at[1 - core], d_all.at[core], pair_s.at[2], pair_r.at[2], "ctx", partner
    )
    keep = pltpu.make_async_copy(d_mine.at[core], d_all.at[core], local_sem.at[4])
    keep.start()
    rank_turned = columns_contract(ob_s[...], cot_all[core]).astype(jnp.bfloat16)
    oa_term = dot(rank_turned, att_s[...]).astype(jnp.bfloat16)
    for unit in range(16):
        high, tile = unit // 8, unit % 8
        xe[unit // 8, unit // 2 % 4, unit % 2] = oa_term[
            16 * high:16 * high + 16, 128 * tile:128 * tile + 128
        ]
    for copy in heads:
        copy.wait_recv()
    oy_s[...] = ox_s[0] + ox_s[1] + ox_s[2] + ox_s[3]
    heads.append(send(oy_s, oz_s, h_s.at[3], h_r.at[3], "head", facing))
    swap_d.wait_recv()
    keep.wait()
    at = (core, row, slot, partner, near, near_at, kin_slot, kin, group_at)
    sent = []

    def backward(pair, total):
        turns, plains = [], []
        for even in range(2):
            number = 2 * pair + even
            lanes = pl.ds(pl.multiple_of(lax.rem(number, 4) * 128, 128), 128)
            d_prob = columns_contract(d_all[number // 4, :, lanes], val_s[number])
            weights = wt_s[number].astype(jnp.float32)
            delta = jnp.sum(weights * d_prob, -1, keepdims=True)
            d_score = (weights * (d_prob - delta) * scale).astype(jnp.bfloat16)
            grad = dot(d_score, kcat_s[number])
            plains.append(grad[:, :128])
            turns.append(turned(grad[:, 128:], cos_ref[...], -sin_ref[...]))
        turn = jnp.where(early, turns[0], turns[1])
        moved = pltpu.roll(plains[1], 64, 1)
        parts = [plains[0], jnp.where(early, turn, moved), jnp.where(early, moved, turn)]
        for i, piece in enumerate(parts):
            at = pl.ds(pl.multiple_of(pair * 384 + i * 128, 128), 128)
            piece = piece.astype(jnp.bfloat16)
            grad_s[:, at] = piece
            total = total + columns_contract(qb_s[:, at], piece)
        return total

    total = lax.fori_loop(0, 2, backward, jnp.zeros((32, 128), jnp.float32))
    heads[3].wait_recv()
    o_low = (oy_s[...] + oz_s[...]).astype(jnp.bfloat16)
    ob_term = dot(o_low, cot_all[core])
    lane = lax.broadcasted_iota(jnp.int32, (32, 128), 1)

    def shifted(start, to):
        tile, offset = start // 128, start % 128
        shift = (to - offset) % 128
        value = pltpu.roll(ob_term[:, 128 * tile:128 * tile + 128], shift, 1)
        if offset + 40 > 128:
            after = pltpu.roll(ob_term[:, 128 * tile + 128:128 * tile + 256], shift, 1)
            value = jnp.where(lane < to + 128 - offset, value, after)
        return value

    for half in range(2):
        for line_row in range(4):
            for third in range(3):
                packed = jnp.zeros((32, 128), jnp.float32)
                for i in range(3):
                    member = 3 * third + i
                    if member > 7:
                        continue
                    value = shifted(40 * (8 * member + 2 * line_row + half), 40 * i)
                    inside = (lane >= 40 * i) & (lane < 40 * i + 40)
                    packed = jnp.where(inside, value, packed)
                packed = packed.astype(jnp.bfloat16)
                xe[half, line_row, 2 + 2 * third] = packed[:16]
                xe[half, line_row, 3 + 2 * third] = packed[16:]

    def tail(total):
        third = lax.rem(slot, 3)
        value = jnp.where(third == 1, pltpu.roll(total, 88, 1), total)
        value = jnp.where(third == 2, pltpu.roll(total, 48, 1), value)
        ob_out[...] = value

    soon = tree_reduce(
        at, xe, re1, te1, re2, te2, re3, ge, full_e, tail,
        tree_s.at[0], tree_r.at[0], None, sent,
    )
    next(soon)
    total = lax.fori_loop(2, 3, backward, total)
    next(soon)
    total = lax.fori_loop(3, 4, backward, total)
    part_s[...] = total
    hx_s[x] = total
    late = [
        send(part_s, hx_s.at[x], h_s.at[4 + i], h_r.at[4 + i], "head", beside[i]) for i in range(3)
    ]
    next(soon)
    qb_term = dot(low_turned, grad_s[...]).astype(jnp.bfloat16)
    for unit in range(24):
        high, tile = unit // 12, unit % 12
        xb[unit // 12, unit // 3 % 4, unit % 3] = qb_term[
            16 * high:16 * high + 16, 128 * tile:128 * tile + 128
        ]
    wide = tree_reduce(
        at, xb, rb1, tb1, rb2, tb2, rb3, gb, full_b, None,
        tree_s.at[1], tree_r.at[1], None, sent,
    )
    next(wide)
    for copy in late:
        copy.wait_recv()
    hy_s[...] = hx_s[0] + hx_s[1] + hx_s[2] + hx_s[3]
    late.append(send(hy_s, hz_s, h_s.at[7], h_r.at[7], "head", facing))
    next(wide)
    next(soon)
    late[3].wait_recv()
    sums = (hy_s[...] + hz_s[...]).astype(jnp.bfloat16)
    qa_term = dot(sums, ql_s[...]).astype(jnp.bfloat16)
    for unit in range(24):
        high, tile = unit // 12, unit % 12
        xa[unit // 12, unit // 3 % 4, unit % 3] = qa_term[
            16 * high:16 * high + 16, 128 * tile:128 * tile + 128
        ]
    slim = tree_reduce(
        at, xa, ra1, ta1, ra2, ta2, ra3, gq, full_a, None,
        tree_s.at[2], tree_r.at[2], None, sent,
    )
    next(slim)
    next(slim)
    next(wide)
    next(slim)
    next(wide)
    next(soon)
    next(slim)
    next(wide)
    next(slim)
    heads += late

    done = first + pending + [swap_w, swap_d] + line[0] + line[1] + line[2] + heads + sent
    for copy in done + across[0] + across[1] + relays + list(rings.values()):
        copy.wait_send()


def finish_kernel(full_e, full_b, full_a, tail_ref, qa_out, qb_out, oa_out, ob_out):
    for source, out, kept in ((full_a, qa_out, 3), (full_b, qb_out, 3), (full_e, oa_out, 2)):
        tiles = out.shape[1] // 128
        for unit in range(8 * kept):
            high, tile = unit // tiles, unit % tiles
            out[16 * high:16 * high + 16, 128 * tile:128 * tile + 128] = source[
                unit // (4 * kept), unit // kept % 4, unit % kept
            ].astype(jnp.float32)
    ob_out[...] = tail_ref[...][:, :40]


def shaped(shape, dtype=jnp.bfloat16):
    return jax.ShapeDtypeStruct(shape, dtype)


def body(
    frozen_queries,
    query_latent_rows,
    key_value_latent,
    block_starts,
    latent_up_weight,
    query_adapter_first,
    query_adapter_second,
    output_adapter_first,
    output_adapter_second,
    frozen_output_weight,
    output_cotangent,
):
    token_rows = frozen_queries.shape[0]
    per_head_width = PLAIN_WIDTH + ROTARY_WIDTH
    head_number = query_adapter_second.shape[1] // per_head_width
    width = output_cotangent.shape[1]
    rank = query_adapter_first.shape[1]
    held_rows, held_columns = frozen_output_weight.shape
    half_out = held_rows // 2
    bf = jnp.bfloat16
    keys = SPAN * token_rows
    plain, turn = head_number * PLAIN_WIDTH, head_number * ROTARY_WIDTH

    def tree(used, kept, deep):
        return [
            VMEM((2, 4, used, 16, 128), bf), VMEM((4, used, 16, 128), bf),
            VMEM((4, used, 16, 128), bf), VMEM((3, used, 16, 128), bf),
            VMEM((8, deep, 16, 128), bf), VMEM((8, deep, 16, 128), bf), VMEM((kept, 16, 128), bf),
        ]

    close, far = pl.BlockSpec(memory_space=VMEM), pl.BlockSpec(memory_space=pltpu.HBM)
    f32 = jnp.float32
    pieces = pl.pallas_call(
        attend_kernel,
        out_shape=(
            shaped((2, 4, 2, 16, 128)),
            shaped((2, 4, 3, 16, 128)),
            shaped((2, 4, 3, 16, 128)),
            shaped((rank, 128), f32),
        ),
        in_specs=[pl.BlockSpec(memory_space=pltpu.SMEM)] + [far] * 10,
        out_specs=(close,) * 4,
        scratch_shapes=[
            VMEM((KVL + ROTARY_WIDTH, token_rows), bf), VMEM((4, token_rows // 4, 640), bf),
            VMEM((8, 128), jnp.int32), VMEM((4, token_rows // 4, 640), bf),
            VMEM((8, 128), jnp.int32), VMEM((128, 128), f32), VMEM((128, 128), f32),
            VMEM((SPAN, 4, token_rows // 4, 640), bf), VMEM((SPAN, 8, 128), jnp.int32),
            VMEM((4, 8, 2, held_columns, half_out), bf), VMEM((2, token_rows, width), bf),
            VMEM((2, token_rows, half_out), bf), VMEM((2, token_rows, half_out), bf),
            VMEM(frozen_queries.shape, bf), VMEM(query_latent_rows.shape, bf),
            VMEM((rank, query_latent_rows.shape[1]), bf), VMEM(query_adapter_second.shape, bf),
            VMEM((rank, held_rows), bf), VMEM((rank, width), bf), VMEM(latent_up_weight.shape, bf),
            VMEM((token_rows, plain), bf), VMEM((token_rows, turn), bf),
            VMEM((head_number, keys, 256), bf), VMEM((head_number, keys, 128), bf),
            VMEM((head_number, token_rows, keys), bf), VMEM((token_rows, held_rows), bf),
            VMEM(frozen_queries.shape, bf),
            VMEM((rank, 128), f32), VMEM((4, rank, 128), f32),
            VMEM((rank, 128), f32), VMEM((rank, 128), f32),
            VMEM((rank, 128), f32), VMEM((4, rank, 128), f32),
            VMEM((rank, 128), f32), VMEM((rank, 128), f32),
            *tree(8, 2, 4), *tree(3, 3, 3), *tree(3, 3, 3),
            DMA((5,)), DMA((7,)), DMA((7,)), DMA((7,)), DMA((7,)), DMA((3,)), DMA((3,)),
            DMA((3, 2)), DMA((3, 2)), DMA((2, 4, 4)), DMA((2, 4, 4)), DMA((2, 8)), DMA((2, 8)),
            DMA((8,)), DMA((8,)), DMA((8,)), DMA((8,)), DMA((3, 18)), DMA((3, 18)), DMA((10,)),
        ],
        compiler_params=pltpu.CompilerParams(
            collective_id=0, has_side_effects=True, vmem_limit_bytes=56 * 1024 * 1024
        ),
    )(
        block_starts, key_value_latent.T,
        frozen_output_weight.T, output_cotangent, frozen_queries, query_latent_rows,
        query_adapter_first.T, query_adapter_second, output_adapter_first.T,
        output_adapter_second, latent_up_weight,
    )
    grad_qa, grad_qb, grad_oa, grad_ob = pl.pallas_call(
        finish_kernel,
        out_shape=(
            shaped((rank, query_latent_rows.shape[1]), f32),
            shaped(query_adapter_second.shape, f32),
            shaped((rank, held_rows), f32),
            shaped((rank, held_columns), f32),
        ),
        in_specs=[close] * 4,
        out_specs=(close,) * 4,
    )(*pieces)
    return (grad_qa.T, grad_qb, grad_oa.T, grad_ob)


def solution(mesh):
    return jax.shard_map(
        body,
        mesh=mesh,
        in_specs=(
            P("ctx", "head"),
            P("ctx", None),
            P("ctx", None),
            P("ctx", None),
            P(None, "head"),
            P(),
            P(None, "head"),
            P("head", None),
            P(),
            P("head", "ctx"),
            P("ctx", None),
        ),
        out_specs=(P(), P(None, "head"), P("head", None), P(None, "ctx")),
        check_vma=False,
    )
```
